256 devices in a mesh: ga: 16 (over z_lo, y), pair: 16 (over z_hi, x, core).
Axes of the slice: x: 4, y: 4, z: 8 (z_hi: 2, z_lo: 4; z = z_hi * 4 + z_lo), core: 2. Of those that a mesh axis runs over, the one named last changes fastest.
Arguments:
- val_density: bfloat16 [256, 3, 2, 8192], P('pair', None, None, 'ga'), may hold values from -0.0625 to 0.0625
- con_density: bfloat16 [576, 3, 2, 8192], P('ga', None, None, 'pair'), may hold values from -6 to 6
- screened: bfloat16 [3, 2, 8192, 8192], P(None, None, 'ga', 'pair'), may hold values from -0.0625 to 0.0625
- coulomb: float32 [3, 8192], P(None, 'ga'), may hold values from 0.2 to 2
- trans_here: bfloat16 [384, 2, 8192], P('pair', None, 'ga'), may hold values from -6 to 6
- trans_there: bfloat16 [384, 3, 2, 8192], P('pair', None, None, 'ga'), may hold values from -0.0625 to 0.0625
- shift_map: int32 [3, 8192], P(None, 'pair'), may hold values from 0 to 8191, as said below
- ordering: int32 [384], replicated, may hold values from 0 to 383, each once
Outputs:
- kernel: float32 [3, 2, 384, 384], P(None, None, 'pair', 'ga')
The draws below stay inside these ranges and needn't reach their ends.
Inputs may be any that keep to these rules, and one draw needn't show every extreme that they name: `shift_map`: each aligned block of 128 entries of a row is a permutation of that block's own G-vector indices.
All inputs are finite; a program needn't handle non-finite values.
Results may differ from the reference program's by a relative error of at most 0.0003.
Values may be sent and summed in bfloat16 or wider, within the bound.
A program may use at most 64 MiB of HBM per device.

```python
import math
import jax
import jax.numpy as jnp
from jax import lax

NV = 16
NC = 24
NG = 8192
GBLK = 128
KSEL = 3
VV = 256
CC = 576
NT = 384


def draw_shift_map(key, part):
    scores = jax.random.randint(jax.random.fold_in(key, 11), (KSEL, NG // GBLK, GBLK), 0, 1 << 20)
    scores = scores * GBLK + jnp.arange(GBLK, dtype=jnp.int32)
    within = jnp.argsort(scores, axis=-1, stable=True).astype(jnp.int32)
    offsets = (jnp.arange(NG // GBLK, dtype=jnp.int32) * GBLK)[None, :, None]
    return (within + offsets).reshape(KSEL, NG)


def level_of(key, dims, cuts, least, largest):
    factor_of, own = 1.0, jax.random.fold_in(key, 6)
    for position, parts in cuts:
        steps = jnp.exp(jax.random.uniform(jax.random.fold_in(own, position), (parts,), jnp.float32, least / len(cuts), largest / len(cuts)))
        factor_of = factor_of * jnp.repeat(steps, dims[position] // parts).reshape([-1 if axis == position else 1 for axis in range(len(dims))])
    return factor_of


def normal_values(key, shape, scale, most, cuts=(), kind=jnp.bfloat16):
    level = level_of(key, shape, cuts, -0.22, 0.18) if cuts else 1.0
    array = jax.random.normal(key, shape, jnp.float32) * scale * level
    return jnp.minimum(jnp.maximum(array, -most), most).astype(kind)


def setup_inputs(seed: int = 0) -> dict:
    arg_keys = jax.random.split(jax.random.key(seed), 9)
    val_density = normal_values(arg_keys[0], (VV, KSEL, 2, NG), NG ** -0.5, 0.0625, ((0, 16), (3, 16)))
    con_density = normal_values(arg_keys[1], (CC, KSEL, 2, NG), 1.0, 6.0, ((0, 16), (3, 16)))
    screened = normal_values(arg_keys[2], (KSEL, 2, NG, NG), NG ** -0.5, 0.0625, ((2, 16), (3, 16)))
    coulomb = jnp.clip(jnp.exp(math.log(2.0) - 2.3025851 * jax.random.uniform(arg_keys[3], (KSEL, NG), jnp.float32) ** level_of(arg_keys[3], (KSEL, NG), ((1, 16),), -0.2, 0.2)), 0.2, 2.0)
    trans_here = normal_values(arg_keys[4], (NT, 2, NG), 1.0, 6.0, ((0, 16), (2, 16)))
    trans_there = normal_values(arg_keys[5], (NT, KSEL, 2, NG), NG ** -0.5, 0.0625, ((0, 16), (3, 16)))
    shift_map = draw_shift_map(jax.random.fold_in(arg_keys[8], 71), 0)
    ordering = jax.random.permutation(arg_keys[7], NT).astype(jnp.int32)
    return dict(val_density=val_density, con_density=con_density, screened=screened, coulomb=coulomb, trans_here=trans_here, trans_there=trans_there, shift_map=shift_map, ordering=ordering)


def complex_rows(left, right):
    high = lax.Precision.HIGHEST
    real_part = jnp.dot(left[0], right[0].T, precision=high) - jnp.dot(left[1], right[1].T, precision=high)
    imag_part = jnp.dot(left[0], right[1].T, precision=high) + jnp.dot(left[1], right[0].T, precision=high)
    return jnp.stack([real_part, imag_part], axis=0)


def reference(val_density, con_density, screened, coulomb, trans_here, trans_there, shift_map, ordering):
    lookup = jnp.broadcast_to(shift_map[None, :, None, :], con_density.shape).astype(jnp.int32)
    shifted = jnp.take_along_axis(con_density, lookup, axis=3).astype(jnp.float32)
    valence = val_density.astype(jnp.float32)
    here = trans_here.astype(jnp.float32)
    there = trans_there.astype(jnp.float32) * coulomb[None, :, None, :]

    def one_point(point):
        weights = screened[point].astype(jnp.float32)
        conduct = jnp.transpose(shifted[:, point], (1, 0, 2))
        screened_rows = jnp.stack([
            jnp.dot(conduct[0], weights[0].T, precision=lax.Precision.HIGHEST) - jnp.dot(conduct[1], weights[1].T, precision=lax.Precision.HIGHEST),
            jnp.dot(conduct[0], weights[1].T, precision=lax.Precision.HIGHEST) + jnp.dot(conduct[1], weights[0].T, precision=lax.Precision.HIGHEST)], axis=0)
        left = jnp.transpose(valence[:, point], (1, 0, 2))
        direct = complex_rows(left, screened_rows)
        outer = jnp.transpose(there[:, point], (1, 0, 2))
        exchange = complex_rows(jnp.transpose(here, (1, 0, 2)), outer)
        return direct, exchange

    direct, exchange = lax.map(one_point, jnp.arange(KSEL, dtype=jnp.int32))
    trans = jnp.arange(NT, dtype=jnp.int32)
    valence_band = trans // NC
    conduct_band = trans % NC
    row_pairs = valence_band[:, None] * NV + valence_band[None, :]
    col_pairs = conduct_band[:, None] * NC + conduct_band[None, :]
    regrouped = direct[:, :, row_pairs, col_pairs]
    natural = 2.0 * exchange - regrouped
    natural = natural[:, :, ordering, :]
    return natural[:, :, :, ordering]
```

```python
import jax
import jax.numpy as jnp
from jax import lax
from jax.sharding import PartitionSpec as P

NV = 16
NC = 24
GBLK = 128
NT = 384
F32 = jnp.float32
BF16 = jnp.bfloat16


def two_terms(values):
    high = lax.reduce_precision(values, exponent_bits=8, mantissa_bits=7)
    low = lax.reduce_precision(values - high, exponent_bits=8, mantissa_bits=7)
    return high.astype(BF16), low.astype(BF16)


def on_device(
    val_density, con_density, screened, coulomb, trans_here, trans_there, shift_map, ordering
):
    con_count, points, _, slab_cols = con_density.shape
    blocks = slab_cols // GBLK
    pairs = lax.axis_size("pair")
    slabs = lax.axis_size("ga")
    whole_con = lax.all_gather(con_density, "ga", axis=0, tiled=True)
    whole_val = lax.all_gather(val_density, "pair", axis=0, tiled=True)
    whole_here = lax.all_gather(trans_here, "pair", axis=0, tiled=True)
    within = (shift_map % GBLK).reshape(points, blocks, GBLK)
    onehot = (
        within[:, :, :, None] == jnp.arange(GBLK, dtype=jnp.int32)[None, None, None, :]
    ).astype(BF16)

    def mul(spec, left, right):
        return jnp.einsum(spec, left, right, preferred_element_type=F32)

    rows_re = mul("akg,kgh->kah", whole_val[:, :, 0], screened[:, 0]) - mul(
        "akg,kgh->kah", whole_val[:, :, 1], screened[:, 1]
    )
    rows_im = mul("akg,kgh->kah", whole_val[:, :, 0], screened[:, 1]) + mul(
        "akg,kgh->kah", whole_val[:, :, 1], screened[:, 0]
    )
    shape = (points, NV * NV, blocks, GBLK)

    def unshift(term):
        moved = mul("kang,kngh->kanh", term.reshape(shape), onehot).astype(BF16)
        return moved.reshape(points, NV * NV, slab_cols)

    real = [unshift(term) for term in two_terms(rows_re)]
    imag = [unshift(term) for term in two_terms(rows_im)]
    left_re = jnp.concatenate([real[0], -imag[0], real[1], -imag[1]], axis=2)
    left_im = jnp.concatenate([imag[0], real[0], imag[1], real[1]], axis=2)
    con_rows = jnp.transpose(whole_con, (1, 0, 2, 3)).reshape(points, NC * NC, 2 * slab_cols)
    con_twice = jnp.concatenate([con_rows, con_rows], axis=2)
    direct = jnp.stack(
        [mul("kax,kbx->kab", left_re, con_twice), mul("kax,kbx->kab", left_im, con_twice)], axis=1
    )
    direct = jnp.transpose(direct.reshape(points, 2, NV, NV, NC * NC), (3, 0, 1, 2, 4))
    direct = lax.psum_scatter(direct, "pair", scatter_dimension=0, tiled=True)[0]
    direct = jnp.transpose(direct.reshape(points, 2, NV, NC, NC), (2, 3, 0, 1, 4)).reshape(
        NT, points, 2, NC
    )
    weighted = trans_there.astype(F32) * coulomb[None, :, None, :]
    high = lax.Precision.HIGHEST
    here = whole_here.astype(F32)
    exch_re = jnp.einsum("tg,skg->tks", here[:, 0], weighted[:, :, 0], precision=high) - jnp.einsum(
        "tg,skg->tks", here[:, 1], weighted[:, :, 1], precision=high
    )
    exch_im = jnp.einsum("tg,skg->tks", here[:, 0], weighted[:, :, 1], precision=high) + jnp.einsum(
        "tg,skg->tks", here[:, 1], weighted[:, :, 0], precision=high
    )
    natural = 2.0 * jnp.stack([exch_re, exch_im], axis=2) - direct
    rows = natural[ordering]
    rows = lax.all_to_all(
        rows.reshape(pairs, NT // pairs, points, 2, NC), "pair", split_axis=0, concat_axis=0
    )
    cols = jnp.transpose(rows, (0, 4, 2, 3, 1)).reshape(NT, points * 2 * (NT // pairs))
    cols = cols[ordering]
    cols = lax.psum_scatter(cols, "ga", scatter_dimension=0, tiled=True)
    cols = cols.reshape(NT // slabs, points, 2, NT // pairs)
    return jnp.transpose(cols, (1, 2, 3, 0))


def solution(mesh):
    in_specs = (
        P("pair", None, None, "ga"),
        P("ga", None, None, "pair"),
        P(None, None, "ga", "pair"),
        P(None, "ga"),
        P("pair", None, "ga"),
        P("pair", None, None, "ga"),
        P(None, "pair"),
        P(),
    )
    out_specs = P(None, None, "pair", "ga")
    return jax.shard_map(
        on_device, mesh=mesh, in_specs=in_specs, out_specs=out_specs, check_vma=False
    )
```

```python
import functools

import jax
import jax.numpy as jnp
from jax import lax
from jax.experimental import pallas as pl
from jax.experimental.pallas import tpu as pltpu
from jax.sharding import PartitionSpec as P

NV = 16
NC = 24
GBLK = 128
NT = 384
KSEL = 3
F32 = jnp.float32
BF16 = jnp.bfloat16
MESH = pl.DeviceIdType.MESH


def position():
    ga, pair = lax.axis_index("ga"), lax.axis_index("pair")
    return dict(
        ga=ga,
        pair=pair,
        zl=lax.div(ga, 4),
        y=lax.rem(ga, 4),
        zh=lax.div(pair, 8),
        x=lax.rem(lax.div(pair, 2), 4),
        core=lax.rem(pair, 2),
    )


def device(at, **moved):
    here = {**at, **moved}
    return (here["zl"] * 4 + here["y"], here["zh"] * 8 + here["x"] * 2 + here["core"])


def greet(peers):
    barrier = pltpu.get_barrier_semaphore()
    for peer in peers:
        pl.semaphore_signal(barrier, inc=1, device_id=peer, device_id_type=MESH)
    pl.semaphore_wait(barrier, len(peers))


def remote(src, dst, send_sem, recv_sem, to):
    return pltpu.make_async_remote_copy(
        src_ref=src, dst_ref=dst, send_sem=send_sem, recv_sem=recv_sem, device_id=to, device_id_type=MESH
    )


def dot(left, right):
    return jnp.dot(left, right, preferred_element_type=F32)


def dot_rows(left, right):
    return lax.dot_general(left, right, (((1,), (1,)), ((), ())), preferred_element_type=F32)


def two_terms(values):
    high = values.astype(BF16)
    return high, (values - high.astype(F32)).astype(BF16)


def tiles_kernel(
    con_in, val_in, here_in, scr_in, there_ref, coul_ref, within_ref,
    part_ref, exch_ref,
    con_all, val_all, here_all, weights, con_rows, left_hi, left_lo, direct, from_core, from_x,
    con_send, con_recv, val_send, val_recv, here_send, here_recv,
    core_send, core_recv, x_send, x_recv, local,
):
    at = position()
    ga, pair, zl, y, zh, x, core = (at[k] for k in ("ga", "pair", "zl", "y", "zh", "x", "core"))
    turn = lambda v, d: lax.rem(v + d, 4)
    other_core = device(at, core=1 - core)
    other_zh = device(at, zh=1 - zh)
    x_peers = [device(at, x=turn(x, d)) for d in (1, 2, 3)]
    z_peers = [device(at, zl=turn(zl, d)) for d in (1, 2, 3)]
    y_next, y_prev = device(at, y=turn(y, 1)), device(at, y=turn(y, 3))

    loads = [pltpu.make_async_copy(scr_in.at[q], weights.at[q], local.at[q]) for q in range(KSEL)]
    loads.append(pltpu.make_async_copy(val_in, val_all.at[pair], local.at[3]))
    loads.append(pltpu.make_async_copy(here_in, here_all.at[pair], local.at[4]))
    loads.append(pltpu.make_async_copy(con_in, con_all.at[ga], local.at[5]))
    for load in loads:
        load.start()
    greet([other_core, other_zh, y_next, y_prev] + x_peers + z_peers)

    pending = []

    def start(copy):
        copy.start()
        pending.append(copy)

    counts = {"con": 0, "val": 0, "here": 0}
    kinds = {
        "val": (val_in, val_all, val_send, val_recv),
        "here": (here_in, here_all, here_send, here_recv),
    }

    def send_pair(kind, owner, to, fresh):
        own, slots, send_sems, recv_sems = kinds[kind]
        src = own if fresh else slots.at[owner]
        start(remote(src, slots.at[owner], send_sems.at[counts[kind]], recv_sems.at[owner], to))
        counts[kind] += 1

    def wait_pair(kind, owner):
        own, slots, send_sems, recv_sems = kinds[kind]
        remote(own, slots.at[owner], send_sems.at[0], recv_sems.at[owner], other_core).wait_recv()

    def send_con(q, owner, to, fresh):
        src = con_in.at[q] if fresh else con_all.at[owner, q]
        start(remote(src, con_all.at[owner, q], con_send.at[counts["con"]], con_recv.at[owner, q], to))
        counts["con"] += 1

    def wait_con(q, owner):
        remote(con_in.at[q], con_all.at[owner, q], con_send.at[0], con_recv.at[owner, q], other_core).wait_recv()

    def pair_at(zh_, x_, core_):
        return zh_ * 8 + x_ * 2 + core_

    def spread_own(kind):
        send_pair(kind, pair, other_zh, True)
        for peer in x_peers:
            send_pair(kind, pair, peer, True)
        send_pair(kind, pair, other_core, True)

    def spread_rest(kind):
        owner = pair_at(1 - zh, x, core)
        wait_pair(kind, owner)
        for peer in x_peers:
            send_pair(kind, owner, peer, False)
        send_pair(kind, owner, other_core, False)
        for zh_ in (zh, 1 - zh):
            for d in (1, 2, 3):
                owner = pair_at(zh_, turn(x, d), core)
                wait_pair(kind, owner)
                send_pair(kind, owner, other_core, False)

    def gather_rest(kind):
        for zh_ in (zh, 1 - zh):
            for d in (0, 1, 2, 3):
                wait_pair(kind, pair_at(zh_, turn(x, d), 1 - core))

    def con_z(q):
        for peer in z_peers:
            send_con(q, ga, peer, True)

    def con_y(q):
        send_con(q, ga, y_next, True)
        send_con(q, ga, y_prev, True)

    def con_from_z(q):
        for d in (1, 3, 2):
            owner = turn(zl, d) * 4 + y
            wait_con(q, owner)
            send_con(q, owner, y_next, False)
            send_con(q, owner, y_prev, False)

    def con_from_y(q):
        for zl_ in (0, 1):
            owner = zl_ * 4 + turn(y, 3)
            wait_con(q, owner)
            send_con(q, owner, y_next, False)
        for zl_ in (2, 3):
            owner = zl_ * 4 + turn(y, 1)
            wait_con(q, owner)
            send_con(q, owner, y_prev, False)

    def con_rest(q):
        for zl_ in (2, 3):
            wait_con(q, zl_ * 4 + turn(y, 3))
        for zl_ in (0, 1):
            wait_con(q, zl_ * 4 + turn(y, 1))
        for zl_ in (0, 1, 2, 3):
            wait_con(q, zl_ * 4 + turn(y, 2))

    def unshift_weights(q):
        loads[q].wait()
        for n in range(4):
            row = within_ref[pl.ds(q * 4 + n, 1), :]
            onehot = (lax.broadcasted_iota(jnp.int32, (GBLK, GBLK), 0) == row).astype(F32).astype(BF16)
            cols = slice(n * GBLK, (n + 1) * GBLK)
            weights[q, :, cols] = dot_rows(weights[q, :, cols], onehot).astype(BF16)

    def rows_of(q):
        to_row = lax.broadcasted_iota(jnp.int32, (NV * NV, NV * NV), 0)
        from_row = lax.broadcasted_iota(jnp.int32, (NV * NV, NV * NV), 1)
        v, place = to_row & 15, to_row >> 4
        w = (place & 1) * 8 + ((place >> 1) & 3) * 2 + (place >> 3)
        order = (from_row == v * NV + w).astype(F32).astype(BF16)
        gathered = val_all[:, q].reshape(NV * NV, 1024)
        val = dot(order, gathered).astype(BF16)
        val_re, val_im = val[:, :512], val[:, 512:]
        scr_re, scr_im = weights[q, :512, :], weights[q, 512:, :]
        real_hi, real_lo = two_terms(dot(val_re, scr_re) - dot(val_im, scr_im))
        imag_hi, imag_lo = two_terms(dot(val_re, scr_im) + dot(val_im, scr_re))
        for ref, real, imag in ((left_hi, real_hi, imag_hi), (left_lo, real_lo, imag_lo)):
            ref[q, 0, :, :512] = real
            ref[q, 0, :, 512:] = -imag
            ref[q, 1, :, :512] = imag
            ref[q, 1, :, 512:] = real

    def contract(q):
        con_rest(q)
        for owner in range(16):
            con_rows[owner * 36 : (owner + 1) * 36, :] = con_all[owner, q]

        @pl.loop(0, 2)
        def _(p):
            direct[q, p] = dot_rows(left_hi[q, p], con_rows[...]) + dot_rows(left_lo[q, p], con_rows[...])

        start(
            remote(
                direct.at[q, :, pl.ds(pl.multiple_of((1 - core) * 128, 128), 128), :],
                from_core.at[q], core_send.at[q], core_recv.at[q], other_core,
            )
        )

    def add_core(q):
        own = pl.ds(pl.multiple_of(core * 128, 128), 128)
        remote(direct.at[q, :, own, :], from_core.at[q], core_send.at[q], core_recv.at[q], other_core).wait_recv()
        for p in range(2):
            direct[q, p, own, :] = direct[q, p, own, :] + from_core[q, p]
        for d in (1, 2, 3):
            rows = pl.ds(pl.multiple_of(core * 128 + turn(x, d) * 32, 32), 32)
            start(
                remote(
                    direct.at[q, :, rows, :], from_x.at[q, d - 1],
                    x_send.at[q, d - 1], x_recv.at[q, d - 1], x_peers[d - 1],
                )
            )

    def add_x(q):
        rows = pl.ds(pl.multiple_of(core * 128 + x * 32, 32), 32)
        for d in (1, 2, 3):
            remote(
                direct.at[q, :, rows, :], from_x.at[q, d - 1],
                x_send.at[q, d - 1], x_recv.at[q, d - 1], x_peers[d - 1],
            ).wait_recv()
        for p in range(2):
            part_ref[q, p] = direct[q, p, rows, :] + from_x[q, 0, p] + from_x[q, 1, p] + from_x[q, 2, p]

    def exchange():
        gather_rest("here")
        loads[4].wait()
        terms = []
        for q in range(KSEL):
            values = there_ref[q].astype(F32) * coul_ref[pl.ds(q, 1), :]
            high, low = two_terms(values)
            for p in range(2):
                for term in (high, low):
                    if p == 0:
                        swapped = jnp.concatenate([term[:, :512], -term[:, 512:]], axis=1)
                    else:
                        swapped = jnp.concatenate([term[:, 512:], term[:, :512]], axis=1)
                    terms.append(swapped)
        highs = jnp.concatenate([t.astype(F32) for t in terms[0::2]], axis=0).astype(BF16)
        lows = jnp.concatenate([t.astype(F32) for t in terms[1::2]], axis=0).astype(BF16)
        for v in range(NV):
            rows = here_all[v]
            exch_ref[v * NC : (v + 1) * NC, :] = dot_rows(rows, highs) + dot_rows(rows, lows)

    spread_own("val")
    con_z(0)
    con_y(0)
    spread_own("here")
    con_z(1)
    con_z(2)
    con_y(1)
    for q in range(KSEL):
        unshift_weights(q)
    spread_rest("val")
    con_from_z(0)
    gather_rest("val")
    loads[3].wait()
    rows_of(0)
    loads[5].wait()
    con_from_y(0)
    con_y(2)
    con_from_z(1)
    spread_rest("here")
    rows_of(1)
    contract(0)
    con_from_y(1)
    con_from_z(2)
    rows_of(2)
    add_core(0)
    contract(1)
    con_from_y(2)
    exchange()
    add_core(1)
    contract(2)
    add_x(0)
    add_core(2)
    add_x(1)
    add_x(2)
    for copy in pending:
        copy.wait_send()


def gather_and_multiply(con, val, here, scr, there, coul, within):
    any_space = pl.BlockSpec(memory_space=pl.ANY)
    vmem = pl.BlockSpec(memory_space=pltpu.VMEM)
    dma = pltpu.SemaphoreType.DMA
    return pl.pallas_call(
        tiles_kernel,
        name="gather_and_multiply",
        out_shape=(
            jax.ShapeDtypeStruct((KSEL, 2, 32, NC * NC), F32),
            jax.ShapeDtypeStruct((NT, KSEL * 2 * NC), F32),
        ),
        in_specs=[any_space] * 4 + [vmem] * 3,
        out_specs=(vmem, vmem),
        scratch_shapes=[
            pltpu.VMEM((16, KSEL, 36, 1024), BF16),
            pltpu.VMEM((16, KSEL, NV, 1024), BF16),
            pltpu.VMEM((16, NC, 1024), BF16),
            pltpu.VMEM((KSEL, 1024, 512), BF16),
            pltpu.VMEM((NC * NC, 1024), BF16),
            pltpu.VMEM((KSEL, 2, NV * NV, 1024), BF16),
            pltpu.VMEM((KSEL, 2, NV * NV, 1024), BF16),
            pltpu.VMEM((KSEL, 2, NV * NV, NC * NC), F32),
            pltpu.VMEM((KSEL, 2, 128, NC * NC), F32),
            pltpu.VMEM((KSEL, 3, 2, 32, NC * NC), F32),
            dma((45,)), dma((16, KSEL)), dma((16,)), dma((16,)), dma((16,)), dma((16,)),
            dma((KSEL,)), dma((KSEL,)), dma((KSEL, 3)), dma((KSEL, 3)), dma((6,)),
        ],
        compiler_params=pltpu.CompilerParams(
            collective_id=0, has_side_effects=True, vmem_limit_bytes=60 * 2**20
        ),
    )(con, val, here, scr, there, coul, within)


def order_kernel(
    part_ref, exch_ref, places_ref, out_ref,
    rows_all, moved, from_x, whole, cols, from_y, slab, from_z,
    x_send, x_recv, y_send, y_recv, z_send, z_recv,
):
    at = position()
    ga, pair, zl, y, zh, x, core = (at[k] for k in ("ga", "pair", "zl", "y", "zh", "x", "core"))
    turn = lambda v, d: lax.rem(v + d, 4)
    z = zh * 4 + zl
    x_steps = [(d, c) for c in (0, 1) for d in range(4) if (d, c) != (0, 0)]
    x_peers = [device(at, x=turn(x, d), core=lax.rem(core + c, 2)) for d, c in x_steps]
    y_peers = [device(at, y=turn(y, d)) for d in (1, 2, 3)]
    z_to = [lax.rem(z + d, 8) for d in range(1, 8)]
    z_peers = [device(at, zh=lax.div(t, 4), zl=lax.rem(t, 4)) for t in z_to]
    greet(x_peers + y_peers + z_peers)
    pending = []

    def start(copy):
        copy.start()
        pending.append(copy)

    places = jnp.transpose(jnp.broadcast_to(places_ref[...].astype(F32), (GBLK, NT)))
    lanes = lax.broadcasted_iota(jnp.int32, (NT, GBLK), 1)
    natural, swapped = [], []
    whole_places = places.astype(jnp.int32)
    band = jnp.zeros((NT, GBLK), jnp.int32)
    for step in range(1, NV):
        band = band + (whole_places >= step * NC).astype(jnp.int32)
    other = (whole_places - band * NC) * NV + band
    for n in range(3):
        natural.append((whole_places == lanes + n * GBLK).astype(F32))
        swapped.append((other == lanes + n * GBLK).astype(F32))
    natural = jnp.concatenate(natural, axis=1).astype(BF16)
    swapped = jnp.concatenate(swapped, axis=1).astype(BF16)

    for half in range(2):
        for q in range(KSEL):
            for p in range(2):
                tile = part_ref[q, p, half * NV : (half + 1) * NV, :]
                lane = half * 144 + (q * 2 + p) * NC
                for c in range(NC):
                    rows_all[c * NV : (c + 1) * NV, lane : lane + NC] = tile[:, c * NC : (c + 1) * NC]
    rows_hi, rows_lo = two_terms(rows_all[...])
    exch_hi, exch_lo = two_terms(exch_ref[...])
    exch = 2.0 * (dot(natural, exch_hi) + dot(natural, exch_lo))
    direct = dot(swapped, rows_hi) + dot(swapped, rows_lo)
    mine = zh.astype(F32)
    moved[:, 0:144] = exch * (1.0 - mine) - direct[:, 0:144]
    moved[:, 144:288] = exch * mine - direct[:, 144:288]

    def row_block(zh_, x_, core_):
        return pl.ds(pl.multiple_of((zh_ * 8 + x_ * 2 + core_) * NC, 8), NC)

    for k, (d, c) in enumerate(x_steps):
        x_, core_ = turn(x, d), lax.rem(core + c, 2)
        for half in range(2):
            start(
                remote(
                    moved.at[row_block(half, x_, core_), :], from_x.at[x * 2 + core, half],
                    x_send.at[k, half], x_recv.at[x * 2 + core, half], x_peers[k],
                )
            )
    for half in range(2):
        from_x[x * 2 + core, half] = moved[row_block(half, x, core), :]
    for k, (d, c) in enumerate(x_steps):
        slot = turn(x, d) * 2 + lax.rem(core + c, 2)
        for half in range(2):
            remote(
                from_x.at[slot, half], from_x.at[slot, half],
                x_send.at[0, half], x_recv.at[slot, half], x_peers[k],
            ).wait_recv()
    for half in range(2):
        for slot in range(8):
            tile = from_x[slot, half]
            for zh_ in range(2):
                w = zh_ * 8 + slot
                for plane in range(6):
                    lane = zh_ * 144 + plane * NC
                    whole[half, plane * NC : (plane + 1) * NC, w * NC : (w + 1) * NC] = tile[:, lane : lane + NC]
        whole_hi, whole_lo = two_terms(whole[half])
        cols[half] = dot_rows(natural, whole_hi) + dot_rows(natural, whole_lo)

    def col_block(zl_, y_):
        return pl.ds(pl.multiple_of((zl_ * 4 + y_) * NC, 8), NC)

    for d in (1, 2, 3):
        for zl_ in range(4):
            start(
                remote(
                    cols.at[:, col_block(zl_, turn(y, d)), :], from_y.at[d - 1, zl_],
                    y_send.at[d - 1, zl_], y_recv.at[d - 1, zl_], y_peers[d - 1],
                )
            )
    for zl_ in range(4):
        for d in (1, 2, 3):
            remote(
                from_y.at[d - 1, zl_], from_y.at[d - 1, zl_],
                y_send.at[d - 1, zl_], y_recv.at[d - 1, zl_], y_peers[d - 1],
            ).wait_recv()
        slab[zl_] = cols[:, col_block(zl_, y), :] + from_y[0, zl_] + from_y[1, zl_] + from_y[2, zl_]
    for d in range(1, 8):
        t = z_to[d - 1]
        start(
            remote(
                slab.at[lax.rem(t, 4), lax.div(t, 4)], from_z.at[d - 1],
                z_send.at[d - 1], z_recv.at[d - 1], z_peers[d - 1],
            )
        )
    for d in range(1, 8):
        remote(
            from_z.at[d - 1], from_z.at[d - 1], z_send.at[d - 1], z_recv.at[d - 1], z_peers[d - 1]
        ).wait_recv()
    total = slab[zl, zh]
    for d in range(7):
        total = total + from_z[d]
    out_ref[...] = total
    for copy in pending:
        copy.wait_send()


def permute_and_sum(part, exch, places):
    vmem = pl.BlockSpec(memory_space=pltpu.VMEM)
    dma = pltpu.SemaphoreType.DMA
    return pl.pallas_call(
        order_kernel,
        name="permute_and_sum",
        out_shape=jax.ShapeDtypeStruct((NC, KSEL * 2 * NC), F32),
        in_specs=[vmem] * 3,
        out_specs=vmem,
        scratch_shapes=[
            pltpu.VMEM((NT, 288), F32),
            pltpu.VMEM((NT, 288), F32),
            pltpu.VMEM((8, 2, NC, 288), F32),
            pltpu.VMEM((2, 144, NT), F32),
            pltpu.VMEM((2, NT, 144), F32),
            pltpu.VMEM((3, 4, 2, NC, 144), F32),
            pltpu.VMEM((4, 2, NC, 144), F32),
            pltpu.VMEM((7, NC, 144), F32),
            dma((7, 2)), dma((8, 2)), dma((3, 4)), dma((3, 4)), dma((7,)), dma((7,)),
        ],
        compiler_params=pltpu.CompilerParams(
            collective_id=1, has_side_effects=True, vmem_limit_bytes=40 * 2**20
        ),
    )(part, exch, places)


def on_device(
    val_density, con_density, screened, coulomb, trans_here, trans_there, shift_map, ordering
):
    con = jnp.transpose(con_density, (1, 0, 2, 3)).reshape(KSEL, 36, 1024)
    val = jnp.transpose(val_density, (1, 0, 2, 3)).reshape(KSEL, NV, 1024)
    there = jnp.transpose(trans_there, (1, 0, 2, 3)).reshape(KSEL, NC, 1024)
    here = trans_here.reshape(NC, 1024)
    scr = screened.reshape(KSEL, 1024, 512)
    coul = jnp.concatenate([coulomb, coulomb], axis=1)
    within = (shift_map % GBLK).reshape(KSEL * 4, GBLK)
    part, exch = gather_and_multiply(con, val, here, scr, there, coul, within)
    cols = permute_and_sum(part, exch, ordering.reshape(1, NT))
    return jnp.transpose(cols.reshape(NC, KSEL, 2, NC), (1, 2, 3, 0))


def solution(mesh):
    in_specs = (
        P("pair", None, None, "ga"),
        P("ga", None, None, "pair"),
        P(None, None, "ga", "pair"),
        P(None, "ga"),
        P("pair", None, "ga"),
        P("pair", None, None, "ga"),
        P(None, "pair"),
        P(),
    )
    out_specs = P(None, None, "pair", "ga")
    return jax.shard_map(
        on_device, mesh=mesh, in_specs=in_specs, out_specs=out_specs, check_vma=False
    )
```

```python
import functools

import jax
import jax.numpy as jnp
from jax import lax
from jax.experimental import pallas as pl
from jax.experimental.pallas import tpu as pltpu
from jax.sharding import PartitionSpec as P

NV = 16
NC = 24
GBLK = 128
NT = 384
KSEL = 3
F32 = jnp.float32
BF16 = jnp.bfloat16
MESH = pl.DeviceIdType.MESH


def position():
    ga, pair = lax.axis_index("ga"), lax.axis_index("pair")
    return dict(
        ga=ga,
        pair=pair,
        zl=lax.div(ga, 4),
        y=lax.rem(ga, 4),
        zh=lax.div(pair, 8),
        x=lax.rem(lax.div(pair, 2), 4),
        core=lax.rem(pair, 2),
    )


def device(at, **moved):
    here = {**at, **moved}
    return (here["zl"] * 4 + here["y"], here["zh"] * 8 + here["x"] * 2 + here["core"])


def greet(peers):
    for peer in peers:
        pl.semaphore_signal(pltpu.get_barrier_semaphore(), inc=1, device_id=peer, device_id_type=MESH)


def remote(src, dst, send_sem, recv_sem, to):
    return pltpu.make_async_remote_copy(
        src_ref=src, dst_ref=dst, send_sem=send_sem, recv_sem=recv_sem, device_id=to, device_id_type=MESH
    )


def dot(left, right):
    return jnp.dot(left, right, preferred_element_type=F32)


def dot_rows(left, right):
    return lax.dot_general(left, right, (((1,), (1,)), ((), ())), preferred_element_type=F32)


def two_terms(values):
    high = values.astype(BF16)
    return high, (values - high.astype(F32)).astype(BF16)


def tiles_kernel(
    con_in, val_in, here_in, there_in, scr_in, coul_ref, shift_ref, places_ref,
    out_ref,
    con_raw, val_raw, here_raw, there_raw,
    con_all, val_all, here_all, here_rows, weights, con_rows, left_hi, left_lo, direct, from_core, from_x,
    rows_sel, cols_sel, exch_moved, parts, moved, from_rows, whole, cols, from_y, slab, from_z,
    con_send, con_recv, val_send, val_recv, here_send, here_recv,
    core_send, core_recv, x_send, x_recv, row_send, row_recv, y_send, y_recv, z_send, z_recv, local,
):
    at = position()
    ga, pair, zl, y, zh, x, core = (at[k] for k in ("ga", "pair", "zl", "y", "zh", "x", "core"))
    turn = lambda v, d: lax.rem(v + d, 4)
    other_core = device(at, core=1 - core)
    other_zh = device(at, zh=1 - zh)
    x_peers = [device(at, x=turn(x, d)) for d in (1, 2, 3)]
    y_peers = [device(at, y=turn(y, d)) for d in (1, 2, 3)]
    y_next, y_prev = y_peers[0], y_peers[2]
    row_steps = [(d, c) for c in (0, 1) for d in range(4) if (d, c) != (0, 0)]
    row_peers = [device(at, x=turn(x, d), core=lax.rem(core + c, 2)) for d, c in row_steps]
    z_to = [lax.rem(zh * 4 + zl + d, 8) for d in range(1, 8)]
    z_peers = [device(at, zh=lax.div(t, 4), zl=lax.rem(t, 4)) for t in z_to]

    loads = [
        pltpu.make_async_copy(src, dst, local.at[k])
        for k, (src, dst) in enumerate(
            [(val_in, val_raw), (con_in, con_raw), (here_in, here_raw), (there_in, there_raw)]
            + [(scr_in.at[q], weights.at[q]) for q in range(KSEL)]
        )
    ]
    for load in loads:
        load.start()
    greet(row_peers + y_peers + z_peers)
    loads[0].wait()
    for q in range(KSEL):
        for p in range(2):
            val_all[pair, q, :, p * 512 : (p + 1) * 512] = val_raw[:, q, p, :]
    loads[1].wait()
    for q in range(KSEL):
        for p in range(2):
            con_all[ga, q, p * 36 : (p + 1) * 36, :] = con_raw[:, q, p, :]
    loads[2].wait()
    for p in range(2):
        here_all[pair, :, p * 512 : (p + 1) * 512] = here_raw[:, p, :]
    pl.semaphore_wait(pltpu.get_barrier_semaphore(), len(row_peers + y_peers + z_peers))

    pending, maybe = [], []
    up, down = device(at, zl=turn(zl, 1)), device(at, zl=turn(zl, 3))

    def start(copy):
        copy.start()
        pending.append(copy)

    counts = {"con": 0, "val": 0, "here": 0}
    kinds = {"val": (val_all, val_send, val_recv), "here": (here_all, here_send, here_recv)}

    def send_pair(kind, owner, to):
        slots, send_sems, recv_sems = kinds[kind]
        start(remote(slots.at[owner], slots.at[owner], send_sems.at[counts[kind]], recv_sems.at[owner], to))
        counts[kind] += 1

    def wait_pair(kind, owner):
        slots, send_sems, recv_sems = kinds[kind]
        remote(slots.at[owner], slots.at[owner], send_sems.at[0], recv_sems.at[owner], other_core).wait_recv()

    def send_con(q, owner, to, when=None):
        slot = con_all.at[owner, q]
        copy = remote(slot, slot, con_send.at[counts["con"]], con_recv.at[owner, q], to)
        counts["con"] += 1
        if when is None:
            start(copy)
        else:
            pl.when(when)(copy.start)
            maybe.append((copy, when))

    def wait_con(q, owner):
        slot = con_all.at[owner, q]
        remote(slot, slot, con_send.at[0], con_recv.at[owner, q], other_core).wait_recv()

    def pair_at(zh_, x_, core_):
        return zh_ * 8 + x_ * 2 + core_

    def spread_own(kind):
        send_pair(kind, pair, other_zh)
        for peer in x_peers:
            send_pair(kind, pair, peer)
        send_pair(kind, pair, other_core)

    def spread_zh(kind):
        owner = pair_at(1 - zh, x, core)
        wait_pair(kind, owner)
        for peer in x_peers:
            send_pair(kind, owner, peer)
        send_pair(kind, owner, other_core)

    def spread_x(kind, zh_):
        for d in (1, 3, 2):
            owner = pair_at(zh_, turn(x, d), core)
            wait_pair(kind, owner)
            send_pair(kind, owner, other_core)

    def gather_rest(kind):
        for zh_ in (zh, 1 - zh):
            for d in (0, 1, 2, 3):
                wait_pair(kind, pair_at(zh_, turn(x, d), 1 - core))

    def con_z(q):
        send_con(q, ga, up, zl < 3)
        send_con(q, ga, down, zl > 0)

    def con_y(q):
        send_con(q, ga, y_next)
        send_con(q, ga, y_prev)

    def con_from_z(q, hops):
        for owner_zl, has, onward, goes in (
            (jnp.maximum(zl - hops, 0), zl >= hops, up, zl < 3),
            (jnp.minimum(zl + hops, 3), zl + hops <= 3, down, zl > 0),
        ):
            owner = owner_zl * 4 + y
            pl.when(has)(functools.partial(wait_con, q, owner))
            if hops < 3:
                send_con(q, owner, onward, jnp.logical_and(has, goes))
            send_con(q, owner, y_next, has)
            send_con(q, owner, y_prev, has)

    def con_from_y(q):
        for zl_ in (0, 1):
            owner = zl_ * 4 + turn(y, 3)
            wait_con(q, owner)
            send_con(q, owner, y_next)
        for zl_ in (2, 3):
            owner = zl_ * 4 + turn(y, 1)
            wait_con(q, owner)
            send_con(q, owner, y_prev)

    def con_rest(q):
        for zl_ in (2, 3):
            wait_con(q, zl_ * 4 + turn(y, 3))
        for zl_ in (0, 1):
            wait_con(q, zl_ * 4 + turn(y, 1))
        for zl_ in (0, 1, 2, 3):
            wait_con(q, zl_ * 4 + turn(y, 2))

    def unshift_weights(q):
        loads[4 + q].wait()
        for n in range(4):
            cols_ = slice(n * GBLK, (n + 1) * GBLK)
            row = shift_ref[pl.ds(q, 1), cols_] & (GBLK - 1)
            onehot = (lax.broadcasted_iota(jnp.int32, (GBLK, GBLK), 0) == row).astype(F32).astype(BF16)
            weights[q, :, cols_] = dot_rows(weights[q, :, cols_], onehot).astype(BF16)

    def rows_of(q):
        to_row = lax.broadcasted_iota(jnp.int32, (NV * NV, NV * NV), 0)
        from_row = lax.broadcasted_iota(jnp.int32, (NV * NV, NV * NV), 1)
        v, place = to_row & 15, to_row >> 4
        w = (place & 1) * 8 + ((place >> 1) & 3) * 2 + (place >> 3)
        order = (from_row == v * NV + w).astype(F32).astype(BF16)
        val = dot(order, val_all[:, q].reshape(NV * NV, 1024)).astype(BF16)
        val_re, val_im = val[:, :512], val[:, 512:]
        scr_re, scr_im = weights[q, :512, :], weights[q, 512:, :]
        real_hi, real_lo = two_terms(dot(val_re, scr_re) - dot(val_im, scr_im))
        imag_hi, imag_lo = two_terms(dot(val_re, scr_im) + dot(val_im, scr_re))
        for ref, real, imag in ((left_hi, real_hi, imag_hi), (left_lo, real_lo, imag_lo)):
            ref[q, 0, :, :512] = real
            ref[q, 0, :, 512:] = -imag
            ref[q, 1, :, :512] = imag
            ref[q, 1, :, 512:] = real

    def core_copy(q):
        other = pl.ds(pl.multiple_of((1 - core) * 128, 128), 128)
        return remote(direct.at[q, :, other, :], from_core.at[q], core_send.at[q], core_recv.at[q], other_core)

    def contract(q):
        con_rest(q)
        for owner in range(16):
            for p in range(2):
                con_rows[owner * 36 : (owner + 1) * 36, p * 512 : (p + 1) * 512] = con_all[
                    owner, q, p * 36 : (p + 1) * 36, :
                ]

        @pl.loop(0, 2)
        def _(p):
            direct[q, p] = dot_rows(left_hi[q, p], con_rows[...]) + dot_rows(left_lo[q, p], con_rows[...])

        start(core_copy(q))

    def x_copy(q, d):
        rows = pl.ds(pl.multiple_of(core * 128 + turn(x, d) * 32, 32), 32)
        return remote(
            direct.at[q, :, rows, :], from_x.at[q, d - 1], x_send.at[q, d - 1], x_recv.at[q, d - 1], x_peers[d - 1]
        )

    def add_core(q):
        core_copy(q).wait_recv()
        own = pl.ds(pl.multiple_of(core * 128, 128), 128)
        for p in range(2):
            direct[q, p, own, :] = direct[q, p, own, :] + from_core[q, p]
        for d in (2, 1, 3):
            start(x_copy(q, d))

    def row_copy(q, k):
        d, c = row_steps[k]
        rows = pl.ds(pl.multiple_of((turn(x, d) * 2 + lax.rem(core + c, 2)) * 48, 8), 48)
        return remote(
            moved.at[q, rows, :], from_rows.at[q, x * 2 + core], row_send.at[q, k], row_recv.at[q, x * 2 + core],
            row_peers[k],
        )

    def permute_rows(q):
        for d in (1, 2, 3):
            x_copy(q, d).wait_recv()
        for p in range(2):
            for half in range(2):
                rows = pl.ds(pl.multiple_of(core * 128 + x * 32 + half * NV, 16), NV)
                block = slice(half * NV, (half + 1) * NV)
                tile = direct[q, p, rows, :] + from_x[q, 0, p, block] + from_x[q, 1, p, block] + from_x[q, 2, p, block]
                lane = half * 48 + p * NC
                for c in range(NC):
                    parts[c * NV : (c + 1) * NV, lane : lane + NC] = tile[:, c * NC : (c + 1) * NC]
        high, low = two_terms(parts[...])
        moved[q] = exch_moved[q] - dot(rows_sel[...], high) - dot(rows_sel[...], low)
        for k in (1, 0, 2, 5, 4, 6, 3):
            start(row_copy(q, k))
        from_rows[q, x * 2 + core] = moved[q, pl.ds(pl.multiple_of((x * 2 + core) * 48, 8), 48), :]

    def y_copy(q, d):
        rows = pl.ds(pl.multiple_of(turn(y, d) * 96, 32), 96)
        return remote(
            cols.at[q, rows, :], from_y.at[q, d - 1], y_send.at[q, d - 1], y_recv.at[q, d - 1], y_peers[d - 1]
        )

    def permute_cols(q):
        for k, (d, c) in enumerate(row_steps):
            slot = from_rows.at[q, turn(x, d) * 2 + lax.rem(core + c, 2)]
            recv = row_recv.at[q, turn(x, d) * 2 + lax.rem(core + c, 2)]
            remote(slot, slot, row_send.at[q, k], recv, row_peers[k]).wait_recv()
        for slot in range(8):
            for half in range(2):
                tile = from_rows[q, slot, half * NC : (half + 1) * NC, :]
                for zh_ in range(2):
                    w = zh_ * 8 + slot
                    for p in range(2):
                        lane, row = zh_ * 48 + p * NC, half * 48 + p * NC
                        whole[row : row + NC, w * NC : (w + 1) * NC] = tile[:, lane : lane + NC]
        high, low = two_terms(whole[...])
        cols[q] = dot_rows(cols_sel[...], high) + dot_rows(cols_sel[...], low)
        for d in (2, 1, 3):
            start(y_copy(q, d))

    def z_copy(q, d):
        rows = pl.ds(pl.multiple_of(lax.rem(z_to[d - 1], 4) * NC, 8), NC)
        return remote(
            slab.at[q, rows, :], from_z.at[q, d - 1], z_send.at[q, d - 1], z_recv.at[q, d - 1], z_peers[d - 1]
        )

    def add_y(q):
        for d in (1, 2, 3):
            y_copy(q, d).wait_recv()
        own = pl.ds(pl.multiple_of(y * 96, 32), 96)
        slab[q] = cols[q, own, :] + from_y[q, 0] + from_y[q, 1] + from_y[q, 2]
        for d in (4, 3, 5, 2, 6, 1, 7):
            start(z_copy(q, d))

    def add_z(q):
        total = slab[q, pl.ds(pl.multiple_of(zl * NC, 8), NC), :]
        for d in range(1, 8):
            z_copy(q, d).wait_recv()
        for d in range(7):
            total = total + from_z[q, d]
        out_ref[q] = jnp.where(zh == 0, total[:, :48], total[:, 48:])

    def select():
        places = jnp.transpose(jnp.broadcast_to(places_ref[...].astype(F32), (GBLK, NT))).astype(jnp.int32)
        lanes = lax.broadcasted_iota(jnp.int32, (NT, GBLK), 1)

        def block(k):
            return places[k * NC : (k + 1) * NC]

        by_rows = jnp.concatenate([block(zh_ * 8 + s) for s in range(8) for zh_ in range(2)], axis=0)
        by_cols = jnp.concatenate([block(zl_ * 4 + y_) for y_ in range(4) for zl_ in range(4)], axis=0)
        band = jnp.zeros((NT, GBLK), jnp.int32)
        for step in range(1, NV):
            band = band + (by_rows >= step * NC).astype(jnp.int32)
        swapped = (by_rows - band * NC) * NV + band

        def onehot(which):
            parts_ = [(which == lanes + n * GBLK).astype(F32) for n in range(3)]
            return jnp.concatenate(parts_, axis=1).astype(BF16)

        rows_sel[...] = onehot(swapped)
        cols_sel[...] = onehot(by_cols)
        return onehot(by_rows)

    def exchange():
        by_rows = select()
        gather_rest("here")
        for v in range(NV):
            here_rows[v * NC : (v + 1) * NC, :] = here_all[v]
        loads[3].wait()
        highs, lows = [], []
        for q in range(KSEL):
            coul = coul_ref[pl.ds(q, 1), :]
            real_hi, real_lo = two_terms(there_raw[:, q, 0, :].astype(F32) * coul)
            imag_hi, imag_lo = two_terms(there_raw[:, q, 1, :].astype(F32) * coul)
            for out, real, imag in ((highs, real_hi, imag_hi), (lows, real_lo, imag_lo)):
                real, imag = real.astype(F32), imag.astype(F32)
                out.append(jnp.concatenate([real, -imag], axis=1))
                out.append(jnp.concatenate([imag, real], axis=1))
        highs = jnp.concatenate(highs, axis=0).astype(BF16)
        lows = jnp.concatenate(lows, axis=0).astype(BF16)
        high, low = two_terms(dot_rows(here_rows[...], highs) + dot_rows(here_rows[...], lows))
        ordered = 2.0 * (dot(by_rows, high) + dot(by_rows, low))
        for q in range(KSEL):
            tile = ordered[:, q * 48 : (q + 1) * 48]
            exch_moved[q, :, 0:48] = jnp.where(zh == 0, tile, 0.0)
            exch_moved[q, :, 48:96] = jnp.where(zh == 1, tile, 0.0)

    spread_own("val")
    for q in range(KSEL):
        con_z(q)
        con_y(q)
    for q in range(KSEL):
        unshift_weights(q)
    con_from_z(0, 1)
    spread_zh("val")
    spread_x("val", zh)
    con_from_z(1, 1)
    con_from_z(0, 2)
    spread_x("val", 1 - zh)
    con_from_z(2, 1)
    con_from_z(1, 2)
    con_from_z(0, 3)
    gather_rest("val")
    rows_of(0)
    con_from_y(0)
    con_from_z(2, 2)
    con_from_z(1, 3)
    spread_own("here")
    rows_of(1)
    contract(0)
    con_from_z(2, 3)
    con_from_y(1)
    rows_of(2)
    spread_zh("here")
    add_core(0)
    spread_x("here", zh)
    contract(1)
    con_from_y(2)
    spread_x("here", 1 - zh)
    add_core(1)
    exchange()
    permute_rows(0)
    permute_cols(0)
    contract(2)
    permute_rows(1)
    add_core(2)
    add_y(0)
    permute_cols(1)
    permute_rows(2)
    add_y(1)
    permute_cols(2)
    add_y(2)
    for q in range(KSEL):
        add_z(q)
    for copy, when in maybe:
        pl.when(when)(copy.wait_send)
    for copy in pending:
        copy.wait_send()


def kernel_tiles(con, val, here, there, scr, coul, shift, places):
    any_space = pl.BlockSpec(memory_space=pl.ANY)
    vmem = pl.BlockSpec(memory_space=pltpu.VMEM)
    dma = pltpu.SemaphoreType.DMA
    return pl.pallas_call(
        tiles_kernel,
        name="kernel_tiles",
        out_shape=jax.ShapeDtypeStruct((KSEL, NC, 2 * NC), F32),
        in_specs=[any_space] * 5 + [vmem] * 3,
        out_specs=vmem,
        scratch_shapes=[
            pltpu.VMEM(con.shape, BF16),
            pltpu.VMEM(val.shape, BF16),
            pltpu.VMEM(here.shape, BF16),
            pltpu.VMEM(there.shape, BF16),
            pltpu.VMEM((16, KSEL, 72, 512), BF16),
            pltpu.VMEM((16, KSEL, NV, 1024), BF16),
            pltpu.VMEM((16, NC, 1024), BF16),
            pltpu.VMEM((NT, 1024), BF16),
            pltpu.VMEM((KSEL, 1024, 512), BF16),
            pltpu.VMEM((NC * NC, 1024), BF16),
            pltpu.VMEM((KSEL, 2, NV * NV, 1024), BF16),
            pltpu.VMEM((KSEL, 2, NV * NV, 1024), BF16),
            pltpu.VMEM((KSEL, 2, NV * NV, NC * NC), F32),
            pltpu.VMEM((KSEL, 2, 128, NC * NC), F32),
            pltpu.VMEM((KSEL, 3, 2, 32, NC * NC), F32),
            pltpu.VMEM((NT, NT), BF16),
            pltpu.VMEM((NT, NT), BF16),
            pltpu.VMEM((KSEL, NT, 96), F32),
            pltpu.VMEM((NT, 96), F32),
            pltpu.VMEM((KSEL, NT, 96), F32),
            pltpu.VMEM((KSEL, 8, 48, 96), F32),
            pltpu.VMEM((96, NT), F32),
            pltpu.VMEM((KSEL, NT, 96), F32),
            pltpu.VMEM((KSEL, 3, 96, 96), F32),
            pltpu.VMEM((KSEL, 96, 96), F32),
            pltpu.VMEM((KSEL, 7, NC, 96), F32),
            dma((72,)), dma((16, KSEL)), dma((16,)), dma((16,)), dma((16,)), dma((16,)),
            dma((KSEL,)), dma((KSEL,)), dma((KSEL, 3)), dma((KSEL, 3)), dma((KSEL, 7)), dma((KSEL, 8)),
            dma((KSEL, 3)), dma((KSEL, 3)), dma((KSEL, 7)), dma((KSEL, 7)), dma((7,)),
        ],
        compiler_params=pltpu.CompilerParams(
            collective_id=0, has_side_effects=True, vmem_limit_bytes=60 * 2**20
        ),
    )(con, val, here, there, scr, coul, shift, places)


def on_device(
    val_density, con_density, screened, coulomb, trans_here, trans_there, shift_map, ordering
):
    tiles = kernel_tiles(
        con_density, val_density, trans_here, trans_there, screened.reshape(KSEL, 1024, 512),
        coulomb, shift_map, ordering.reshape(1, NT),
    )
    return jnp.transpose(tiles.reshape(KSEL, NC, 2, NC), (0, 2, 3, 1))


def solution(mesh):
    in_specs = (
        P("pair", None, None, "ga"),
        P("ga", None, None, "pair"),
        P(None, None, "ga", "pair"),
        P(None, "ga"),
        P("pair", None, "ga"),
        P("pair", None, None, "ga"),
        P(None, "pair"),
        P(),
    )
    out_specs = P(None, None, "pair", "ga")
    return jax.shard_map(
        on_device, mesh=mesh, in_specs=in_specs, out_specs=out_specs, check_vma=False
    )
```

```python
import functools

import jax
import jax.numpy as jnp
from jax import lax
from jax.experimental import pallas as pl
from jax.experimental.pallas import tpu as pltpu
from jax.sharding import PartitionSpec as P

NV = 16
NC = 24
GBLK = 128
NT = 384
KSEL = 3
F32 = jnp.float32
BF16 = jnp.bfloat16
MESH = pl.DeviceIdType.MESH


def position():
    ga, pair = lax.axis_index("ga"), lax.axis_index("pair")
    return dict(
        ga=ga,
        pair=pair,
        zl=lax.div(ga, 4),
        y=lax.rem(ga, 4),
        zh=lax.div(pair, 8),
        x=lax.rem(lax.div(pair, 2), 4),
        core=lax.rem(pair, 2),
    )


def device(at, **moved):
    here = {**at, **moved}
    return (here["zl"] * 4 + here["y"], here["zh"] * 8 + here["x"] * 2 + here["core"])


def greet(peers):
    for peer in peers:
        pl.semaphore_signal(pltpu.get_barrier_semaphore(), inc=1, device_id=peer, device_id_type=MESH)


def remote(src, dst, send_sem, recv_sem, to):
    return pltpu.make_async_remote_copy(
        src_ref=src, dst_ref=dst, send_sem=send_sem, recv_sem=recv_sem, device_id=to, device_id_type=MESH
    )


def dot(left, right):
    return jnp.dot(left, right, preferred_element_type=F32)


def dot_rows(left, right):
    return lax.dot_general(left, right, (((1,), (1,)), ((), ())), preferred_element_type=F32)


def two_terms(values):
    high = values.astype(BF16)
    return high, (values - high.astype(F32)).astype(BF16)


def tiles_kernel(
    con_in, val_in, here_in, there_in, scr_in, coul_ref, shift_ref, places_ref,
    out_ref,
    con_raw, val_raw, here_raw, there_raw,
    con_all, val_all, here_all, here_rows, weights, con_rows, left_hi, left_lo, direct, from_core, from_x,
    rows_sel, cols_sel, exch_moved, parts, moved, from_rows, whole, cols, from_y, slab, from_z,
    con_send, con_recv, val_send, val_recv, here_send, here_recv,
    core_send, core_recv, x_send, x_recv, row_send, row_recv, y_send, y_recv, z_send, z_recv, local,
):
    at = position()
    ga, pair, zl, y, zh, x, core = (at[k] for k in ("ga", "pair", "zl", "y", "zh", "x", "core"))
    turn = lambda v, d: lax.rem(v + d, 4)
    other_core = device(at, core=1 - core)
    other_zh = device(at, zh=1 - zh)
    x_peers = [device(at, x=turn(x, d)) for d in (1, 2, 3)]
    y_peers = [device(at, y=turn(y, d)) for d in (1, 2, 3)]
    y_next, y_prev = y_peers[0], y_peers[2]
    row_steps = [(d, c) for c in (0, 1) for d in range(4) if (d, c) != (0, 0)]
    row_peers = [device(at, x=turn(x, d), core=lax.rem(core + c, 2)) for d, c in row_steps]
    z_to = [lax.rem(zh * 4 + zl + d, 8) for d in range(1, 8)]
    z_peers = [device(at, zh=lax.div(t, 4), zl=lax.rem(t, 4)) for t in z_to]

    loads = [
        pltpu.make_async_copy(src, dst, local.at[k])
        for k, (src, dst) in enumerate(
            [(val_in, val_raw), (con_in, con_raw), (here_in, here_raw), (there_in, there_raw)]
            + [(scr_in.at[q], weights.at[q]) for q in range(KSEL)]
        )
    ]
    for load in loads:
        load.start()
    greet(row_peers + y_peers + z_peers)
    loads[0].wait()
    for q in range(KSEL):
        for p in range(2):
            val_all[q, pair, :, p * 512 : (p + 1) * 512] = val_raw[:, q, p, :]
    loads[1].wait()
    for q in range(KSEL):
        for p in range(2):
            con_all[ga, q, p * 36 : (p + 1) * 36, :] = con_raw[:, q, p, :]
    loads[2].wait()
    for p in range(2):
        here_all[pair, :, p * 512 : (p + 1) * 512] = here_raw[:, p, :]
    pl.semaphore_wait(pltpu.get_barrier_semaphore(), len(row_peers + y_peers + z_peers))

    pending, maybe = [], []
    up, down = device(at, zl=turn(zl, 1)), device(at, zl=turn(zl, 3))

    def start(copy):
        copy.start()
        pending.append(copy)

    kinds = {q: (val_all.at[q], val_send.at[q], val_recv.at[q]) for q in range(KSEL)}
    kinds["here"] = (here_all, here_send, here_recv)
    counts = dict.fromkeys(["con", *kinds], 0)

    def send_pair(kind, owner, to):
        slots, send_sems, recv_sems = kinds[kind]
        start(remote(slots.at[owner], slots.at[owner], send_sems.at[counts[kind]], recv_sems.at[owner], to))
        counts[kind] += 1

    def wait_pair(kind, owner):
        slots, send_sems, recv_sems = kinds[kind]
        remote(slots.at[owner], slots.at[owner], send_sems.at[0], recv_sems.at[owner], other_core).wait_recv()

    def send_con(q, owner, to, when=None):
        slot = con_all.at[owner, q]
        copy = remote(slot, slot, con_send.at[counts["con"]], con_recv.at[owner, q], to)
        counts["con"] += 1
        if when is None:
            start(copy)
        else:
            pl.when(when)(copy.start)
            maybe.append((copy, when))

    def wait_con(q, owner):
        slot = con_all.at[owner, q]
        remote(slot, slot, con_send.at[0], con_recv.at[owner, q], other_core).wait_recv()

    def pair_at(zh_, x_, core_):
        return zh_ * 8 + x_ * 2 + core_

    def spread_own(kind):
        send_pair(kind, pair, other_zh)
        for peer in x_peers:
            send_pair(kind, pair, peer)
        send_pair(kind, pair, other_core)

    def spread_zh(kind):
        owner = pair_at(1 - zh, x, core)
        wait_pair(kind, owner)
        for peer in x_peers:
            send_pair(kind, owner, peer)
        send_pair(kind, owner, other_core)

    def spread_x(kind, zh_):
        for d in (1, 3, 2):
            owner = pair_at(zh_, turn(x, d), core)
            wait_pair(kind, owner)
            send_pair(kind, owner, other_core)

    def gather_rest(kind):
        for zh_ in (zh, 1 - zh):
            for d in (0, 1, 2, 3):
                wait_pair(kind, pair_at(zh_, turn(x, d), 1 - core))

    def con_z(q):
        send_con(q, ga, up, zl < 3)
        send_con(q, ga, down, zl > 0)

    near, far = jnp.maximum(zl - 1, 1 - zl), 3 - 3 * lax.div(zl, 2)
    line = (near, 6 - zl - near - far, far)

    def con_line(q):
        for zl_ in line:
            send_con(q, ga, device(at, zl=zl_))

    def con_from_line(q, k):
        owner = line[k] * 4 + y
        wait_con(q, owner)
        send_con(q, owner, y_next)
        send_con(q, owner, y_prev)

    def con_y(q):
        send_con(q, ga, y_next)
        send_con(q, ga, y_prev)

    def con_from_z(q, hops):
        for owner_zl, has, onward, goes in (
            (jnp.maximum(zl - hops, 0), zl >= hops, up, zl < 3),
            (jnp.minimum(zl + hops, 3), zl + hops <= 3, down, zl > 0),
        ):
            owner = owner_zl * 4 + y
            pl.when(has)(functools.partial(wait_con, q, owner))
            if hops < 3:
                send_con(q, owner, onward, jnp.logical_and(has, goes))
            send_con(q, owner, y_next, has)
            send_con(q, owner, y_prev, has)

    def con_from_y(q):
        for zl_ in (0, 1):
            owner = zl_ * 4 + turn(y, 3)
            wait_con(q, owner)
            send_con(q, owner, y_next)
        for zl_ in (2, 3):
            owner = zl_ * 4 + turn(y, 1)
            wait_con(q, owner)
            send_con(q, owner, y_prev)

    def con_rest(q):
        for zl_ in (2, 3):
            wait_con(q, zl_ * 4 + turn(y, 3))
        for zl_ in (0, 1):
            wait_con(q, zl_ * 4 + turn(y, 1))
        for zl_ in (0, 1, 2, 3):
            wait_con(q, zl_ * 4 + turn(y, 2))

    def unshift_weights(q):
        loads[4 + q].wait()
        for n in range(4):
            cols_ = slice(n * GBLK, (n + 1) * GBLK)
            row = shift_ref[pl.ds(q, 1), cols_] & (GBLK - 1)
            onehot = (lax.broadcasted_iota(jnp.int32, (GBLK, GBLK), 0) == row).astype(F32).astype(BF16)
            weights[q, :, cols_] = dot_rows(weights[q, :, cols_], onehot).astype(BF16)

    def rows_of(q):
        to_row = lax.broadcasted_iota(jnp.int32, (NV * NV, NV * NV), 0)
        from_row = lax.broadcasted_iota(jnp.int32, (NV * NV, NV * NV), 1)
        v, place = to_row & 15, to_row >> 4
        w = (place & 1) * 8 + ((place >> 1) & 3) * 2 + (place >> 3)
        order = (from_row == v * NV + w).astype(F32).astype(BF16)
        val = dot(order, val_all[q].reshape(NV * NV, 1024)).astype(BF16)
        val_re, val_im = val[:, :512], val[:, 512:]
        scr_re, scr_im = weights[q, :512, :], weights[q, 512:, :]
        real_hi, real_lo = two_terms(dot(val_re, scr_re) - dot(val_im, scr_im))
        imag_hi, imag_lo = two_terms(dot(val_re, scr_im) + dot(val_im, scr_re))
        for ref, real, imag in ((left_hi, real_hi, imag_hi), (left_lo, real_lo, imag_lo)):
            ref[q, 0, :, :512] = real
            ref[q, 0, :, 512:] = -imag
            ref[q, 1, :, :512] = imag
            ref[q, 1, :, 512:] = real

    def core_copy(q, p):
        other = pl.ds(pl.multiple_of((1 - core) * 128, 128), 128)
        return remote(
            direct.at[q, p, other, :], from_core.at[q, p], core_send.at[q, p], core_recv.at[q, p], other_core
        )

    def contract(q):
        con_rest(q)
        for owner in range(16):
            for p in range(2):
                con_rows[owner * 36 : (owner + 1) * 36, p * 512 : (p + 1) * 512] = con_all[
                    owner, q, p * 36 : (p + 1) * 36, :
                ]
        for p in range(2):
            direct[q, p] = dot_rows(left_hi[q, p], con_rows[...]) + dot_rows(left_lo[q, p], con_rows[...])
            start(core_copy(q, p))

    def x_copy(q, p, slot, rows_for, to):
        rows = pl.ds(pl.multiple_of(core * 128 + turn(x, rows_for) * 32, 32), 32)
        return remote(
            direct.at[q, p, rows, :], from_x.at[q, slot, p],
            x_send.at[q, p, slot], x_recv.at[q, p, slot], x_peers[to - 1],
        )

    def to_each(q, p, d):
        return x_copy(q, p, d - 1, d, d)

    def to_side(q, p, side):
        return x_copy(q, p, side, 3 if side else 1, 3 if side else 1)

    def by_side(q, p):
        return x_copy(q, p, 2, 2, 3 if p else 1)

    def add_core(q):
        own = pl.ds(pl.multiple_of(core * 128, 128), 128)
        for p in range(2):
            core_copy(q, p).wait_recv()
            direct[q, p, own, :] = direct[q, p, own, :] + from_core[q, p]
            if q == 2:
                for d in (2, 1, 3):
                    start(to_each(q, p, d))
            else:
                start(by_side(q, p))
        if q < 2:
            for p in range(2):
                start(to_side(q, p, 1 - p))

    def relay(q):
        for p in range(2):
            by_side(q, p).wait_recv()
            rows = pl.ds(pl.multiple_of(core * 128 + turn(x, 3 if p else 1) * 32, 32), 32)
            direct[q, p, rows, :] = direct[q, p, rows, :] + from_x[q, 2, p]
            start(to_side(q, p, p))

    def row_copy(q, k):
        d, c = row_steps[k]
        rows = pl.ds(pl.multiple_of((turn(x, d) * 2 + lax.rem(core + c, 2)) * 48, 8), 48)
        return remote(
            moved.at[q, rows, :], from_rows.at[q, x * 2 + core], row_send.at[q, k], row_recv.at[q, x * 2 + core],
            row_peers[k],
        )

    def permute_rows(q):
        for p in range(2):
            for copy in [to_each(q, p, d) for d in (1, 2, 3)] if q == 2 else [to_side(q, p, k) for k in (0, 1)]:
                copy.wait_recv()
            for half in range(2):
                rows = pl.ds(pl.multiple_of(core * 128 + x * 32 + half * NV, 16), NV)
                block = slice(half * NV, (half + 1) * NV)
                tile = direct[q, p, rows, :] + from_x[q, 0, p, block] + from_x[q, 1, p, block]
                if q == 2:
                    tile = tile + from_x[q, 2, p, block]
                lane = half * 48 + p * NC
                for c in range(NC):
                    parts[c * NV : (c + 1) * NV, lane : lane + NC] = tile[:, c * NC : (c + 1) * NC]
        high, low = two_terms(parts[...])
        moved[q] = exch_moved[q] - dot(rows_sel[...], high) - dot(rows_sel[...], low)
        for k in (1, 0, 2, 5, 4, 6, 3):
            start(row_copy(q, k))
        from_rows[q, x * 2 + core] = moved[q, pl.ds(pl.multiple_of((x * 2 + core) * 48, 8), 48), :]

    def y_copy(q, d):
        rows = pl.ds(pl.multiple_of(turn(y, d) * 96, 32), 96)
        return remote(
            cols.at[q, rows, :], from_y.at[q, d - 1], y_send.at[q, d - 1], y_recv.at[q, d - 1], y_peers[d - 1]
        )

    def permute_cols(q):
        for k, (d, c) in enumerate(row_steps):
            slot = from_rows.at[q, turn(x, d) * 2 + lax.rem(core + c, 2)]
            recv = row_recv.at[q, turn(x, d) * 2 + lax.rem(core + c, 2)]
            remote(slot, slot, row_send.at[q, k], recv, row_peers[k]).wait_recv()
        for slot in range(8):
            for half in range(2):
                tile = from_rows[q, slot, half * NC : (half + 1) * NC, :]
                for zh_ in range(2):
                    w = zh_ * 8 + slot
                    for p in range(2):
                        lane, row = zh_ * 48 + p * NC, half * 48 + p * NC
                        whole[row : row + NC, w * NC : (w + 1) * NC] = tile[:, lane : lane + NC]
        high, low = two_terms(whole[...])
        cols[q] = dot_rows(cols_sel[...], high) + dot_rows(cols_sel[...], low)
        for d in (2, 1, 3):
            start(y_copy(q, d))

    def z_copy(q, d):
        rows = pl.ds(pl.multiple_of(lax.rem(z_to[d - 1], 4) * NC, 8), NC)
        return remote(
            slab.at[q, rows, :], from_z.at[q, d - 1], z_send.at[q, d - 1], z_recv.at[q, d - 1], z_peers[d - 1]
        )

    def add_y(q):
        for d in (1, 2, 3):
            y_copy(q, d).wait_recv()
        own = pl.ds(pl.multiple_of(y * 96, 32), 96)
        slab[q] = cols[q, own, :] + from_y[q, 0] + from_y[q, 1] + from_y[q, 2]
        for d in (4, 3, 5, 2, 6, 1, 7):
            start(z_copy(q, d))

    def add_z(q):
        total = slab[q, pl.ds(pl.multiple_of(zl * NC, 8), NC), :]
        for d in range(1, 8):
            z_copy(q, d).wait_recv()
        for d in range(7):
            total = total + from_z[q, d]
        out_ref[:, q * 48 : (q + 1) * 48] = jnp.where(zh == 0, total[:, :48], total[:, 48:])

    def select():
        places = jnp.transpose(jnp.broadcast_to(places_ref[...].astype(F32)[None, :], (GBLK, NT))).astype(jnp.int32)
        lanes = lax.broadcasted_iota(jnp.int32, (NT, GBLK), 1)

        def block(k):
            return places[k * NC : (k + 1) * NC]

        by_rows = jnp.concatenate([block(zh_ * 8 + s) for s in range(8) for zh_ in range(2)], axis=0)
        by_cols = jnp.concatenate([block(zl_ * 4 + y_) for y_ in range(4) for zl_ in range(4)], axis=0)
        band = jnp.zeros((NT, GBLK), jnp.int32)
        for step in range(1, NV):
            band = band + (by_rows >= step * NC).astype(jnp.int32)
        swapped = (by_rows - band * NC) * NV + band

        def onehot(which):
            parts_ = [(which == lanes + n * GBLK).astype(F32) for n in range(3)]
            return jnp.concatenate(parts_, axis=1).astype(BF16)

        rows_sel[...] = onehot(swapped)
        cols_sel[...] = onehot(by_cols)
        return onehot(by_rows)

    def exchange():
        by_rows = select()
        gather_rest("here")
        for v in range(NV):
            here_rows[v * NC : (v + 1) * NC, :] = here_all[v]
        loads[3].wait()
        highs, lows = [], []
        for q in range(KSEL):
            coul = coul_ref[pl.ds(q, 1), :]
            real_hi, real_lo = two_terms(there_raw[:, q, 0, :].astype(F32) * coul)
            imag_hi, imag_lo = two_terms(there_raw[:, q, 1, :].astype(F32) * coul)
            for out, real, imag in ((highs, real_hi, imag_hi), (lows, real_lo, imag_lo)):
                real, imag = real.astype(F32), imag.astype(F32)
                out.append(jnp.concatenate([real, -imag], axis=1))
                out.append(jnp.concatenate([imag, real], axis=1))
        highs = jnp.concatenate(highs, axis=0).astype(BF16)
        lows = jnp.concatenate(lows, axis=0).astype(BF16)
        high, low = two_terms(dot_rows(here_rows[...], highs) + dot_rows(here_rows[...], lows))
        ordered = 2.0 * (dot(by_rows, high) + dot(by_rows, low))
        for q in range(KSEL):
            tile = ordered[:, q * 48 : (q + 1) * 48]
            exch_moved[q, :, 0:48] = jnp.where(zh == 0, tile, 0.0)
            exch_moved[q, :, 48:96] = jnp.where(zh == 1, tile, 0.0)

    spread_own(0)
    con_line(0)
    con_y(0)
    con_y(1)
    con_y(2)
    unshift_weights(0)
    con_from_line(0, 0)
    con_z(1)
    spread_zh(0)
    con_from_line(0, 1)
    spread_own(1)
    spread_x(0, zh)
    con_from_line(0, 2)
    con_z(2)
    spread_own(2)
    spread_x(0, 1 - zh)
    con_from_z(1, 1)
    spread_own("here")
    gather_rest(0)
    rows_of(0)
    con_from_y(0)
    spread_zh(1)
    con_from_z(1, 2)
    con_from_z(2, 1)
    spread_x(1, zh)
    spread_zh(2)
    spread_x(1, 1 - zh)
    con_from_z(1, 3)
    spread_x(2, zh)
    spread_zh("here")
    contract(0)
    con_from_y(1)
    con_from_z(2, 2)
    add_core(0)
    spread_x(2, 1 - zh)
    spread_x("here", zh)
    con_from_z(2, 3)
    unshift_weights(1)
    unshift_weights(2)
    spread_x("here", 1 - zh)
    gather_rest(1)
    rows_of(1)
    gather_rest(2)
    rows_of(2)
    exchange()
    relay(0)
    con_from_y(2)
    contract(1)
    add_core(1)
    permute_rows(0)
    contract(2)
    relay(1)
    add_core(2)
    permute_rows(1)
    permute_cols(0)
    permute_rows(2)
    add_y(0)
    permute_cols(1)
    permute_cols(2)
    add_y(1)
    add_z(0)
    add_y(2)
    add_z(1)
    add_z(2)
    for copy, when in maybe:
        pl.when(when)(copy.wait_send)
    for copy in pending:
        copy.wait_send()


def kernel_tiles(con, val, here, there, scr, coul, shift, places):
    any_space = pl.BlockSpec(memory_space=pl.ANY)
    vmem = pl.BlockSpec(memory_space=pltpu.VMEM)
    dma = pltpu.SemaphoreType.DMA
    return pl.pallas_call(
        tiles_kernel,
        name="kernel_tiles",
        out_shape=jax.ShapeDtypeStruct((NC, KSEL * 2 * NC), F32),
        in_specs=[any_space] * 5 + [vmem] * 3,
        out_specs=vmem,
        scratch_shapes=[
            pltpu.VMEM(con.shape, BF16),
            pltpu.VMEM(val.shape, BF16),
            pltpu.VMEM(here.shape, BF16),
            pltpu.VMEM(there.shape, BF16),
            pltpu.VMEM((16, KSEL, 72, 512), BF16),
            pltpu.VMEM((KSEL, 16, NV, 1024), BF16),
            pltpu.VMEM((16, NC, 1024), BF16),
            pltpu.VMEM((NT, 1024), BF16),
            pltpu.VMEM((KSEL, 1024, 512), BF16),
            pltpu.VMEM((NC * NC, 1024), BF16),
            pltpu.VMEM((KSEL, 2, NV * NV, 1024), BF16),
            pltpu.VMEM((KSEL, 2, NV * NV, 1024), BF16),
            pltpu.VMEM((KSEL, 2, NV * NV, NC * NC), F32),
            pltpu.VMEM((KSEL, 2, 128, NC * NC), F32),
            pltpu.VMEM((KSEL, 3, 2, 32, NC * NC), F32),
            pltpu.VMEM((NT, NT), BF16),
            pltpu.VMEM((NT, NT), BF16),
            pltpu.VMEM((KSEL, NT, 96), F32),
            pltpu.VMEM((NT, 96), F32),
            pltpu.VMEM((KSEL, NT, 96), F32),
            pltpu.VMEM((KSEL, 8, 48, 96), F32),
            pltpu.VMEM((96, NT), F32),
            pltpu.VMEM((KSEL, NT, 96), F32),
            pltpu.VMEM((KSEL, 3, 96, 96), F32),
            pltpu.VMEM((KSEL, 96, 96), F32),
            pltpu.VMEM((KSEL, 7, NC, 96), F32),
            dma((72,)), dma((16, KSEL)), dma((KSEL, 16)), dma((KSEL, 16)), dma((16,)), dma((16,)),
            dma((KSEL, 2)), dma((KSEL, 2)), dma((KSEL, 2, 3)), dma((KSEL, 2, 3)), dma((KSEL, 7)), dma((KSEL, 8)),
            dma((KSEL, 3)), dma((KSEL, 3)), dma((KSEL, 7)), dma((KSEL, 7)), dma((7,)),
        ],
        compiler_params=pltpu.CompilerParams(
            collective_id=0, has_side_effects=True, vmem_limit_bytes=60 * 2**20
        ),
    )(con, val, here, there, scr, coul, shift, places)


def on_device(
    val_density, con_density, screened, coulomb, trans_here, trans_there, shift_map, ordering
):
    tiles = kernel_tiles(
        con_density, val_density, trans_here, trans_there, screened.reshape(KSEL, 1024, 512),
        coulomb, shift_map, ordering,
    )
    return jnp.transpose(tiles.reshape(NC, KSEL, 2, NC), (1, 2, 3, 0))


def solution(mesh):
    in_specs = (
        P("pair", None, None, "ga"),
        P("ga", None, None, "pair"),
        P(None, None, "ga", "pair"),
        P(None, "ga"),
        P("pair", None, "ga"),
        P("pair", None, None, "ga"),
        P(None, "pair"),
        P(),
    )
    out_specs = P(None, None, "pair", "ga")
    return jax.shard_map(
        on_device, mesh=mesh, in_specs=in_specs, out_specs=out_specs, check_vma=False
    )
```

```python
import functools

import jax
import jax.numpy as jnp
from jax import lax
from jax.experimental import pallas as pl
from jax.experimental.pallas import tpu as pltpu
from jax.sharding import PartitionSpec as P

NV = 16
NC = 24
GBLK = 128
NT = 384
KSEL = 3
F32 = jnp.float32
BF16 = jnp.bfloat16
MESH = pl.DeviceIdType.MESH


def position():
    ga, pair = lax.axis_index("ga"), lax.axis_index("pair")
    return dict(
        ga=ga,
        pair=pair,
        zl=lax.div(ga, 4),
        y=lax.rem(ga, 4),
        zh=lax.div(pair, 8),
        x=lax.rem(lax.div(pair, 2), 4),
        core=lax.rem(pair, 2),
    )


def device(at, **moved):
    here = {**at, **moved}
    return (here["zl"] * 4 + here["y"], here["zh"] * 8 + here["x"] * 2 + here["core"])


def greet(peers):
    for peer in peers:
        pl.semaphore_signal(pltpu.get_barrier_semaphore(), inc=1, device_id=peer, device_id_type=MESH)


def remote(src, dst, send_sem, recv_sem, to):
    return pltpu.make_async_remote_copy(
        src_ref=src, dst_ref=dst, send_sem=send_sem, recv_sem=recv_sem, device_id=to, device_id_type=MESH
    )


def dot(left, right):
    return jnp.dot(left, right, preferred_element_type=F32)


def dot_rows(left, right):
    return lax.dot_general(left, right, (((1,), (1,)), ((), ())), preferred_element_type=F32)


def two_terms(values):
    high = values.astype(BF16)
    return high, (values - high.astype(F32)).astype(BF16)


def tiles_kernel(
    con_in, val_in, here_in, there_in, scr_in, coul_ref, shift_ref, places_ref,
    out_ref,
    con_raw, val_raw, here_raw, there_raw,
    con_all, val_all, here_all, here_rows, weights, con_rows, left_hi, left_lo, direct, from_core, from_x,
    rows_sel, cols_sel, exch_moved, parts, moved, from_rows, whole, cols, from_y, slab, from_z,
    con_send, con_recv, val_send, val_recv, here_send, here_recv,
    core_send, core_recv, x_send, x_recv, row_send, row_recv, y_send, y_recv, z_send, z_recv, local,
):
    at = position()
    ga, pair, zl, y, zh, x, core = (at[k] for k in ("ga", "pair", "zl", "y", "zh", "x", "core"))
    turn = lambda v, d: lax.rem(v + d, 4)
    other_core = device(at, core=1 - core)
    other_zh = device(at, zh=1 - zh)
    x_peers = [device(at, x=turn(x, d)) for d in (1, 2, 3)]
    y_peers = [device(at, y=turn(y, d)) for d in (1, 2, 3)]
    y_next, y_prev = y_peers[0], y_peers[2]
    row_steps = [(d, c) for c in (0, 1) for d in range(4) if (d, c) != (0, 0)]
    row_peers = [device(at, x=turn(x, d), core=lax.rem(core + c, 2)) for d, c in row_steps]
    z_to = [lax.rem(zh * 4 + zl + d, 8) for d in range(1, 8)]
    z_peers = [device(at, zh=lax.div(t, 4), zl=lax.rem(t, 4)) for t in z_to]

    loads = [
        pltpu.make_async_copy(src, dst, local.at[k])
        for k, (src, dst) in enumerate(
            [(val_in, val_raw), (con_in, con_raw), (here_in, here_raw), (there_in, there_raw)]
            + [(scr_in.at[q], weights.at[q]) for q in range(KSEL)]
        )
    ]
    for load in loads:
        load.start()
    greet(row_peers + y_peers + z_peers)
    loads[0].wait()
    for q in range(KSEL):
        for p in range(2):
            val_all[q, pair, :, p * 512 : (p + 1) * 512] = val_raw[:, q, p, :]
    loads[1].wait()
    for q in range(KSEL):
        for p in range(2):
            con_all[ga, q, p * 36 : (p + 1) * 36, :] = con_raw[:, q, p, :]
    loads[2].wait()
    for p in range(2):
        here_all[pair, :, p * 512 : (p + 1) * 512] = here_raw[:, p, :]
    pl.semaphore_wait(pltpu.get_barrier_semaphore(), len(row_peers + y_peers + z_peers))

    pending, maybe = [], []
    up, down = device(at, zl=turn(zl, 1)), device(at, zl=turn(zl, 3))

    def start(copy):
        copy.start()
        pending.append(copy)

    kinds = {q: (val_all.at[q], val_send.at[q], val_recv.at[q]) for q in range(KSEL)}
    kinds["here"] = (here_all, here_send, here_recv)
    counts = dict.fromkeys(["con", *kinds], 0)

    def send_pair(kind, owner, to):
        slots, send_sems, recv_sems = kinds[kind]
        start(remote(slots.at[owner], slots.at[owner], send_sems.at[counts[kind]], recv_sems.at[owner], to))
        counts[kind] += 1

    def wait_pair(kind, owner):
        slots, send_sems, recv_sems = kinds[kind]
        remote(slots.at[owner], slots.at[owner], send_sems.at[0], recv_sems.at[owner], other_core).wait_recv()

    def send_con(q, owner, to, when=None):
        slot = con_all.at[owner, q]
        copy = remote(slot, slot, con_send.at[counts["con"]], con_recv.at[owner, q], to)
        counts["con"] += 1
        if when is None:
            start(copy)
        else:
            pl.when(when)(copy.start)
            maybe.append((copy, when))

    def wait_con(q, owner):
        slot = con_all.at[owner, q]
        remote(slot, slot, con_send.at[0], con_recv.at[owner, q], other_core).wait_recv()

    def pair_at(zh_, x_, core_):
        return zh_ * 8 + x_ * 2 + core_

    def spread_own(kind):
        send_pair(kind, pair, other_zh)
        for peer in x_peers:
            send_pair(kind, pair, peer)
        send_pair(kind, pair, other_core)

    def spread_zh(kind):
        owner = pair_at(1 - zh, x, core)
        wait_pair(kind, owner)
        for peer in x_peers:
            send_pair(kind, owner, peer)
        send_pair(kind, owner, other_core)

    def spread_x(kind, zh_):
        for d in (1, 3, 2):
            owner = pair_at(zh_, turn(x, d), core)
            wait_pair(kind, owner)
            send_pair(kind, owner, other_core)

    def gather_rest(kind):
        for zh_ in (zh, 1 - zh):
            for d in (0, 1, 2, 3):
                wait_pair(kind, pair_at(zh_, turn(x, d), 1 - core))

    def con_z(q):
        send_con(q, ga, up, zl < 3)
        send_con(q, ga, down, zl > 0)

    near, far = jnp.maximum(zl - 1, 1 - zl), 3 - 3 * lax.div(zl, 2)
    line = (near, 6 - zl - near - far, far)

    def con_line(q):
        for zl_ in line:
            send_con(q, ga, device(at, zl=zl_))

    def con_from_line(q, k):
        owner = line[k] * 4 + y
        wait_con(q, owner)
        send_con(q, owner, y_next)
        send_con(q, owner, y_prev)

    def con_y(q):
        send_con(q, ga, y_next)
        send_con(q, ga, y_prev)

    def con_from_z(q, hops):
        for owner_zl, has, onward, goes in (
            (jnp.maximum(zl - hops, 0), zl >= hops, up, zl < 3),
            (jnp.minimum(zl + hops, 3), zl + hops <= 3, down, zl > 0),
        ):
            owner = owner_zl * 4 + y
            pl.when(has)(functools.partial(wait_con, q, owner))
            if hops < 3:
                send_con(q, owner, onward, jnp.logical_and(has, goes))
            send_con(q, owner, y_next, has)
            send_con(q, owner, y_prev, has)

    def con_from_y(q):
        for zl_ in (0, 1):
            owner = zl_ * 4 + turn(y, 3)
            wait_con(q, owner)
            send_con(q, owner, y_next)
        for zl_ in (2, 3):
            owner = zl_ * 4 + turn(y, 1)
            wait_con(q, owner)
            send_con(q, owner, y_prev)

    def con_rest(q):
        for zl_ in (2, 3):
            wait_con(q, zl_ * 4 + turn(y, 3))
        for zl_ in (0, 1):
            wait_con(q, zl_ * 4 + turn(y, 1))
        for zl_ in (0, 1, 2, 3):
            wait_con(q, zl_ * 4 + turn(y, 2))

    def unshift_weights(q):
        loads[4 + q].wait()
        for n in range(4):
            cols_ = slice(n * GBLK, (n + 1) * GBLK)
            row = shift_ref[pl.ds(q, 1), cols_] & (GBLK - 1)
            onehot = (lax.broadcasted_iota(jnp.int32, (GBLK, GBLK), 0) == row).astype(F32).astype(BF16)
            weights[q, :, cols_] = dot_rows(weights[q, :, cols_], onehot).astype(BF16)

    def rows_of(q):
        to_row = lax.broadcasted_iota(jnp.int32, (NV * NV, NV * NV), 0)
        from_row = lax.broadcasted_iota(jnp.int32, (NV * NV, NV * NV), 1)
        v, place = to_row & 15, to_row >> 4
        w = (place & 1) * 8 + ((place >> 1) & 3) * 2 + (place >> 3)
        order = (from_row == v * NV + w).astype(F32).astype(BF16)
        val = dot(order, val_all[q].reshape(NV * NV, 1024)).astype(BF16)
        val_re, val_im = val[:, :512], val[:, 512:]
        scr_re, scr_im = weights[q, :512, :], weights[q, 512:, :]
        real_hi, real_lo = two_terms(dot(val_re, scr_re) - dot(val_im, scr_im))
        imag_hi, imag_lo = two_terms(dot(val_re, scr_im) + dot(val_im, scr_re))
        for ref, real, imag in ((left_hi, real_hi, imag_hi), (left_lo, real_lo, imag_lo)):
            ref[q, 0, :, :512] = real
            ref[q, 0, :, 512:] = -imag
            ref[q, 1, :, :512] = imag
            ref[q, 1, :, 512:] = real

    def core_copy(q, p):
        other = pl.ds(pl.multiple_of((1 - core) * 128, 128), 128)
        return remote(
            direct.at[q, p, other, :], from_core.at[q, p], core_send.at[q, p], core_recv.at[q, p], other_core
        )

    def contract(q):
        con_rest(q)
        for owner in range(16):
            for p in range(2):
                con_rows[owner * 36 : (owner + 1) * 36, p * 512 : (p + 1) * 512] = con_all[
                    owner, q, p * 36 : (p + 1) * 36, :
                ]
        for p in range(2):
            direct[q, p] = dot_rows(left_hi[q, p], con_rows[...]) + dot_rows(left_lo[q, p], con_rows[...])
            start(core_copy(q, p))

    def x_copy(q, p, slot, rows_for, to):
        rows = pl.ds(pl.multiple_of(core * 128 + turn(x, rows_for) * 32, 32), 32)
        return remote(
            direct.at[q, p, rows, :], from_x.at[q, slot, p],
            x_send.at[q, p, slot], x_recv.at[q, p, slot], x_peers[to - 1],
        )

    def to_side(q, p, side):
        return x_copy(q, p, side, 3 if side else 1, 3 if side else 1)

    def by_side(q, p):
        return x_copy(q, p, 2, 2, 3 if p else 1)

    def add_core(q):
        own = pl.ds(pl.multiple_of(core * 128, 128), 128)
        for p in range(2):
            core_copy(q, p).wait_recv()
            direct[q, p, own, :] = direct[q, p, own, :] + from_core[q, p]
            start(by_side(q, p))
        for p in range(2):
            start(to_side(q, p, 1 - p))

    def relay(q):
        for p in range(2):
            by_side(q, p).wait_recv()
            rows = pl.ds(pl.multiple_of(core * 128 + turn(x, 3 if p else 1) * 32, 32), 32)
            direct[q, p, rows, :] = direct[q, p, rows, :] + from_x[q, 2, p]
            start(to_side(q, p, p))

    def row_copy(q, k):
        d, c = row_steps[k]
        rows = pl.ds(pl.multiple_of((turn(x, d) * 2 + lax.rem(core + c, 2)) * 48, 8), 48)
        return remote(
            moved.at[q, rows, :], from_rows.at[q, x * 2 + core], row_send.at[q, k], row_recv.at[q, x * 2 + core],
            row_peers[k],
        )

    def permute_rows(q):
        for p in range(2):
            for copy in [to_side(q, p, k) for k in (0, 1)]:
                copy.wait_recv()
            for half in range(2):
                rows = pl.ds(pl.multiple_of(core * 128 + x * 32 + half * NV, 16), NV)
                block = slice(half * NV, (half + 1) * NV)
                tile = direct[q, p, rows, :] + from_x[q, 0, p, block] + from_x[q, 1, p, block]
                lane = half * 48 + p * NC
                for c in range(NC):
                    parts[c * NV : (c + 1) * NV, lane : lane + NC] = tile[:, c * NC : (c + 1) * NC]
        high, low = two_terms(parts[...])
        moved[q] = exch_moved[q] - dot(rows_sel[...], high) - dot(rows_sel[...], low)
        for k in (1, 0, 2, 5, 4, 6, 3):
            start(row_copy(q, k))
        from_rows[q, x * 2 + core] = moved[q, pl.ds(pl.multiple_of((x * 2 + core) * 48, 8), 48), :]

    def y_copy(q, d):
        rows = pl.ds(pl.multiple_of(turn(y, d) * 96, 32), 96)
        return remote(
            cols.at[q, rows, :], from_y.at[q, d - 1], y_send.at[q, d - 1], y_recv.at[q, d - 1], y_peers[d - 1]
        )

    def permute_cols(q):
        for k, (d, c) in enumerate(row_steps):
            slot = from_rows.at[q, turn(x, d) * 2 + lax.rem(core + c, 2)]
            recv = row_recv.at[q, turn(x, d) * 2 + lax.rem(core + c, 2)]
            remote(slot, slot, row_send.at[q, k], recv, row_peers[k]).wait_recv()
        for slot in range(8):
            for half in range(2):
                tile = from_rows[q, slot, half * NC : (half + 1) * NC, :]
                for zh_ in range(2):
                    w = zh_ * 8 + slot
                    for p in range(2):
                        lane, row = zh_ * 48 + p * NC, half * 48 + p * NC
                        whole[row : row + NC, w * NC : (w + 1) * NC] = tile[:, lane : lane + NC]
        high, low = two_terms(whole[...])
        cols[q] = dot_rows(cols_sel[...], high) + dot_rows(cols_sel[...], low)
        for d in (2, 1, 3):
            start(y_copy(q, d))

    def z_copy(q, d):
        rows = pl.ds(pl.multiple_of(lax.rem(z_to[d - 1], 4) * NC, 8), NC)
        return remote(
            slab.at[q, rows, :], from_z.at[q, d - 1], z_send.at[q, d - 1], z_recv.at[q, d - 1], z_peers[d - 1]
        )

    def add_y(q):
        for d in (1, 2, 3):
            y_copy(q, d).wait_recv()
        own = pl.ds(pl.multiple_of(y * 96, 32), 96)
        slab[q] = cols[q, own, :] + from_y[q, 0] + from_y[q, 1] + from_y[q, 2]
        for d in (4, 3, 5, 2, 6, 1, 7):
            start(z_copy(q, d))

    def add_z(q):
        total = slab[q, pl.ds(pl.multiple_of(zl * NC, 8), NC), :]
        for d in range(1, 8):
            z_copy(q, d).wait_recv()
        for d in range(7):
            total = total + from_z[q, d]
        out_ref[:, q * 48 : (q + 1) * 48] = jnp.where(zh == 0, total[:, :48], total[:, 48:])

    def select():
        places = jnp.transpose(jnp.broadcast_to(places_ref[...].astype(F32)[None, :], (GBLK, NT))).astype(jnp.int32)
        lanes = lax.broadcasted_iota(jnp.int32, (NT, GBLK), 1)

        def block(k):
            return places[k * NC : (k + 1) * NC]

        by_rows = jnp.concatenate([block(zh_ * 8 + s) for s in range(8) for zh_ in range(2)], axis=0)
        by_cols = jnp.concatenate([block(zl_ * 4 + y_) for y_ in range(4) for zl_ in range(4)], axis=0)
        band = jnp.zeros((NT, GBLK), jnp.int32)
        for step in range(1, NV):
            band = band + (by_rows >= step * NC).astype(jnp.int32)
        swapped = (by_rows - band * NC) * NV + band

        def onehot(which):
            parts_ = [(which == lanes + n * GBLK).astype(F32) for n in range(3)]
            return jnp.concatenate(parts_, axis=1).astype(BF16)

        rows_sel[...] = onehot(swapped)
        cols_sel[...] = onehot(by_cols)
        return onehot(by_rows)

    def exchange():
        by_rows = select()
        gather_rest("here")
        for v in range(NV):
            here_rows[v * NC : (v + 1) * NC, :] = here_all[v]
        loads[3].wait()
        highs, lows = [], []
        for q in range(KSEL):
            coul = coul_ref[pl.ds(q, 1), :]
            real_hi, real_lo = two_terms(there_raw[:, q, 0, :].astype(F32) * coul)
            imag_hi, imag_lo = two_terms(there_raw[:, q, 1, :].astype(F32) * coul)
            for out, real, imag in ((highs, real_hi, imag_hi), (lows, real_lo, imag_lo)):
                real, imag = real.astype(F32), imag.astype(F32)
                out.append(jnp.concatenate([real, -imag], axis=1))
                out.append(jnp.concatenate([imag, real], axis=1))
        highs = jnp.concatenate(highs, axis=0).astype(BF16)
        lows = jnp.concatenate(lows, axis=0).astype(BF16)
        high, low = two_terms(dot_rows(here_rows[...], highs) + dot_rows(here_rows[...], lows))
        ordered = 2.0 * (dot(by_rows, high) + dot(by_rows, low))
        for q in range(KSEL):
            tile = ordered[:, q * 48 : (q + 1) * 48]
            exch_moved[q, :, 0:48] = jnp.where(zh == 0, tile, 0.0)
            exch_moved[q, :, 48:96] = jnp.where(zh == 1, tile, 0.0)

    spread_own(0)
    con_line(0)
    con_z(1)
    con_y(0)
    con_y(1)
    con_y(2)
    unshift_weights(0)
    con_from_line(0, 0)
    spread_zh(0)
    con_from_line(0, 1)
    spread_own(1)
    spread_x(0, zh)
    con_from_line(0, 2)
    con_z(2)
    spread_own(2)
    spread_x(0, 1 - zh)
    con_from_z(1, 1)
    spread_own("here")
    gather_rest(0)
    rows_of(0)
    con_from_y(0)
    spread_zh(1)
    con_from_z(1, 2)
    con_from_z(2, 1)
    spread_x(1, zh)
    spread_zh(2)
    spread_x(1, 1 - zh)
    con_from_z(1, 3)
    spread_x(2, zh)
    spread_zh("here")
    contract(0)
    con_from_y(1)
    con_from_z(2, 2)
    add_core(0)
    spread_x(2, 1 - zh)
    spread_x("here", zh)
    con_from_z(2, 3)
    unshift_weights(1)
    unshift_weights(2)
    spread_x("here", 1 - zh)
    gather_rest(1)
    rows_of(1)
    gather_rest(2)
    rows_of(2)
    exchange()
    relay(0)
    con_from_y(2)
    contract(1)
    add_core(1)
    permute_rows(0)
    contract(2)
    relay(1)
    add_core(2)
    permute_cols(0)
    relay(2)
    permute_rows(1)
    permute_rows(2)
    add_y(0)
    permute_cols(1)
    permute_cols(2)
    add_y(1)
    add_z(0)
    add_y(2)
    add_z(1)
    add_z(2)
    for copy, when in maybe:
        pl.when(when)(copy.wait_send)
    for copy in pending:
        copy.wait_send()


def kernel_tiles(con, val, here, there, scr, coul, shift, places):
    any_space = pl.BlockSpec(memory_space=pl.ANY)
    vmem = pl.BlockSpec(memory_space=pltpu.VMEM)
    dma = pltpu.SemaphoreType.DMA
    return pl.pallas_call(
        tiles_kernel,
        name="kernel_tiles",
        out_shape=jax.ShapeDtypeStruct((NC, KSEL * 2 * NC), F32),
        in_specs=[any_space] * 5 + [vmem] * 3,
        out_specs=vmem,
        scratch_shapes=[
            pltpu.VMEM(con.shape, BF16),
            pltpu.VMEM(val.shape, BF16),
            pltpu.VMEM(here.shape, BF16),
            pltpu.VMEM(there.shape, BF16),
            pltpu.VMEM((16, KSEL, 72, 512), BF16),
            pltpu.VMEM((KSEL, 16, NV, 1024), BF16),
            pltpu.VMEM((16, NC, 1024), BF16),
            pltpu.VMEM((NT, 1024), BF16),
            pltpu.VMEM((KSEL, 1024, 512), BF16),
            pltpu.VMEM((NC * NC, 1024), BF16),
            pltpu.VMEM((KSEL, 2, NV * NV, 1024), BF16),
            pltpu.VMEM((KSEL, 2, NV * NV, 1024), BF16),
            pltpu.VMEM((KSEL, 2, NV * NV, NC * NC), F32),
            pltpu.VMEM((KSEL, 2, 128, NC * NC), F32),
            pltpu.VMEM((KSEL, 3, 2, 32, NC * NC), F32),
            pltpu.VMEM((NT, NT), BF16),
            pltpu.VMEM((NT, NT), BF16),
            pltpu.VMEM((KSEL, NT, 96), F32),
            pltpu.VMEM((NT, 96), F32),
            pltpu.VMEM((KSEL, NT, 96), F32),
            pltpu.VMEM((KSEL, 8, 48, 96), F32),
            pltpu.VMEM((96, NT), F32),
            pltpu.VMEM((KSEL, NT, 96), F32),
            pltpu.VMEM((KSEL, 3, 96, 96), F32),
            pltpu.VMEM((KSEL, 96, 96), F32),
            pltpu.VMEM((KSEL, 7, NC, 96), F32),
            dma((72,)), dma((16, KSEL)), dma((KSEL, 16)), dma((KSEL, 16)), dma((16,)), dma((16,)),
            dma((KSEL, 2)), dma((KSEL, 2)), dma((KSEL, 2, 3)), dma((KSEL, 2, 3)), dma((KSEL, 7)), dma((KSEL, 8)),
            dma((KSEL, 3)), dma((KSEL, 3)), dma((KSEL, 7)), dma((KSEL, 7)), dma((7,)),
        ],
        compiler_params=pltpu.CompilerParams(
            collective_id=0, has_side_effects=True, vmem_limit_bytes=60 * 2**20
        ),
    )(con, val, here, there, scr, coul, shift, places)


def on_device(
    val_density, con_density, screened, coulomb, trans_here, trans_there, shift_map, ordering
):
    tiles = kernel_tiles(
        con_density, val_density, trans_here, trans_there, screened.reshape(KSEL, 1024, 512),
        coulomb, shift_map, ordering,
    )
    return jnp.transpose(tiles.reshape(NC, KSEL, 2, NC), (1, 2, 3, 0))


def solution(mesh):
    in_specs = (
        P("pair", None, None, "ga"),
        P("ga", None, None, "pair"),
        P(None, None, "ga", "pair"),
        P(None, "ga"),
        P("pair", None, "ga"),
        P("pair", None, None, "ga"),
        P(None, "pair"),
        P(),
    )
    out_specs = P(None, None, "pair", "ga")
    return jax.shard_map(
        on_device, mesh=mesh, in_specs=in_specs, out_specs=out_specs, check_vma=False
    )
```

```python
import functools

import jax
import jax.numpy as jnp
from jax import lax
from jax.experimental import pallas as pl
from jax.experimental.pallas import tpu as pltpu
from jax.sharding import PartitionSpec as P

NV = 16
NC = 24
GBLK = 128
NT = 384
KSEL = 3
F32 = jnp.float32
BF16 = jnp.bfloat16
MESH = pl.DeviceIdType.MESH


def position():
    ga, pair = lax.axis_index("ga"), lax.axis_index("pair")
    return dict(
        ga=ga,
        pair=pair,
        zl=lax.div(ga, 4),
        y=lax.rem(ga, 4),
        zh=lax.div(pair, 8),
        x=lax.rem(lax.div(pair, 2), 4),
        core=lax.rem(pair, 2),
    )


def device(at, **moved):
    here = {**at, **moved}
    return (here["zl"] * 4 + here["y"], here["zh"] * 8 + here["x"] * 2 + here["core"])


def greet(peers):
    for peer in peers:
        pl.semaphore_signal(pltpu.get_barrier_semaphore(), inc=1, device_id=peer, device_id_type=MESH)


def remote(src, dst, send_sem, recv_sem, to):
    return pltpu.make_async_remote_copy(
        src_ref=src, dst_ref=dst, send_sem=send_sem, recv_sem=recv_sem, device_id=to, device_id_type=MESH
    )


def dot(left, right):
    return jnp.dot(left, right, preferred_element_type=F32)


def dot_rows(left, right):
    return lax.dot_general(left, right, (((1,), (1,)), ((), ())), preferred_element_type=F32)


def two_terms(values):
    high = values.astype(BF16)
    return high, (values - high.astype(F32)).astype(BF16)


def tiles_kernel(
    con_in, val_in, here_in, there_in, scr_in, coul_ref, shift_ref, places_ref,
    out_ref,
    con_raw, val_raw, here_raw, there_raw,
    con_all, val_all, here_all, here_rows, weights, con_rows, left_hi, left_lo, direct, from_core, from_x,
    rows_sel, cols_sel, exch_moved, parts, moved, from_rows, whole, cols, from_y, slab, from_z,
    con_send, con_recv, val_send, val_recv, here_send, here_recv,
    core_send, core_recv, x_send, x_recv, row_send, row_recv, y_send, y_recv, z_send, z_recv, local,
):
    at = position()
    ga, pair, zl, y, zh, x, core = (at[k] for k in ("ga", "pair", "zl", "y", "zh", "x", "core"))
    turn = lambda v, d: lax.rem(v + d, 4)
    other_core = device(at, core=1 - core)
    other_zh = device(at, zh=1 - zh)
    x_peers = [device(at, x=turn(x, d)) for d in (1, 2, 3)]
    y_peers = [device(at, y=turn(y, d)) for d in (1, 2, 3)]
    y_next, y_prev = y_peers[0], y_peers[2]
    row_steps = [(d, c) for c in (0, 1) for d in range(4) if (d, c) != (0, 0)]
    row_peers = [device(at, x=turn(x, d), core=lax.rem(core + c, 2)) for d, c in row_steps]
    z_to = [lax.rem(zh * 4 + zl + d, 8) for d in range(1, 8)]
    z_peers = [device(at, zh=lax.div(t, 4), zl=lax.rem(t, 4)) for t in z_to]

    loads = [
        pltpu.make_async_copy(src, dst, local.at[k])
        for k, (src, dst) in enumerate(
            [(val_in, val_raw), (con_in, con_raw), (here_in, here_raw), (there_in, there_raw)]
            + [(scr_in.at[q], weights.at[q]) for q in range(KSEL)]
        )
    ]
    for load in loads:
        load.start()
    greet(row_peers + y_peers + z_peers)
    loads[0].wait()
    for q in range(KSEL):
        for p in range(2):
            val_all[q, pair, :, p * 512 : (p + 1) * 512] = val_raw[:, q, p, :]
    loads[1].wait()
    for q in range(KSEL):
        for p in range(2):
            con_all[ga, q, p * 36 : (p + 1) * 36, :] = con_raw[:, q, p, :]
    loads[2].wait()
    for p in range(2):
        here_all[pair, :, p * 512 : (p + 1) * 512] = here_raw[:, p, :]
    pl.semaphore_wait(pltpu.get_barrier_semaphore(), len(row_peers + y_peers + z_peers))

    pending, maybe = [], []
    up, down = device(at, zl=turn(zl, 1)), device(at, zl=turn(zl, 3))

    def start(copy):
        copy.start()
        pending.append(copy)

    kinds = {q: (val_all.at[q], val_send.at[q], val_recv.at[q]) for q in range(KSEL)}
    kinds["here"] = (here_all, here_send, here_recv)
    counts = dict.fromkeys(["con", *kinds], 0)

    def send_pair(kind, owner, to):
        slots, send_sems, recv_sems = kinds[kind]
        start(remote(slots.at[owner], slots.at[owner], send_sems.at[counts[kind]], recv_sems.at[owner], to))
        counts[kind] += 1

    def wait_pair(kind, owner):
        slots, send_sems, recv_sems = kinds[kind]
        remote(slots.at[owner], slots.at[owner], send_sems.at[0], recv_sems.at[owner], other_core).wait_recv()

    def send_con(q, owner, to, when=None):
        slot = con_all.at[owner, q]
        copy = remote(slot, slot, con_send.at[counts["con"]], con_recv.at[owner, q], to)
        counts["con"] += 1
        if when is None:
            start(copy)
        else:
            pl.when(when)(copy.start)
            maybe.append((copy, when))

    def wait_con(q, owner):
        slot = con_all.at[owner, q]
        remote(slot, slot, con_send.at[0], con_recv.at[owner, q], other_core).wait_recv()

    def pair_at(zh_, x_, core_):
        return zh_ * 8 + x_ * 2 + core_

    def spread_own(kind):
        send_pair(kind, pair, other_zh)
        for peer in x_peers:
            send_pair(kind, pair, peer)
        send_pair(kind, pair, other_core)

    def spread_zh(kind):
        owner = pair_at(1 - zh, x, core)
        wait_pair(kind, owner)
        for peer in x_peers:
            send_pair(kind, owner, peer)
        send_pair(kind, owner, other_core)

    def spread_x(kind, zh_):
        for d in (1, 3, 2):
            owner = pair_at(zh_, turn(x, d), core)
            wait_pair(kind, owner)
            send_pair(kind, owner, other_core)

    def gather_rest(kind):
        for zh_ in (zh, 1 - zh):
            for d in (0, 1, 2, 3):
                wait_pair(kind, pair_at(zh_, turn(x, d), 1 - core))

    def con_z(q):
        send_con(q, ga, up, zl < 3)
        send_con(q, ga, down, zl > 0)

    near, far = jnp.maximum(zl - 1, 1 - zl), 3 - 3 * lax.div(zl, 2)
    line = (near, 6 - zl - near - far, far)

    def con_line(q):
        for zl_ in line:
            send_con(q, ga, device(at, zl=zl_))

    def con_from_line(q, k):
        owner = line[k] * 4 + y
        wait_con(q, owner)
        send_con(q, owner, y_next)
        send_con(q, owner, y_prev)

    def con_y(q):
        send_con(q, ga, y_next)
        send_con(q, ga, y_prev)

    def con_from_z(q, hops):
        for owner_zl, has, onward, goes in (
            (jnp.maximum(zl - hops, 0), zl >= hops, up, zl < 3),
            (jnp.minimum(zl + hops, 3), zl + hops <= 3, down, zl > 0),
        ):
            owner = owner_zl * 4 + y
            pl.when(has)(functools.partial(wait_con, q, owner))
            if hops < 3:
                send_con(q, owner, onward, jnp.logical_and(has, goes))
            send_con(q, owner, y_next, has)
            send_con(q, owner, y_prev, has)

    def con_from_y(q):
        for zl_ in (0, 1):
            owner = zl_ * 4 + turn(y, 3)
            wait_con(q, owner)
            send_con(q, owner, y_next)
        for zl_ in (2, 3):
            owner = zl_ * 4 + turn(y, 1)
            wait_con(q, owner)
            send_con(q, owner, y_prev)

    def con_rest(q):
        for zl_ in (2, 3):
            wait_con(q, zl_ * 4 + turn(y, 3))
        for zl_ in (0, 1):
            wait_con(q, zl_ * 4 + turn(y, 1))
        for zl_ in (0, 1, 2, 3):
            wait_con(q, zl_ * 4 + turn(y, 2))

    def unshift_weights(q):
        loads[4 + q].wait()
        for n in range(4):
            cols_ = slice(n * GBLK, (n + 1) * GBLK)
            row = shift_ref[pl.ds(q, 1), cols_] & (GBLK - 1)
            onehot = (lax.broadcasted_iota(jnp.int32, (GBLK, GBLK), 0) == row).astype(F32).astype(BF16)
            weights[q, :, cols_] = dot_rows(weights[q, :, cols_], onehot).astype(BF16)

    def rows_of(q):
        to_row = lax.broadcasted_iota(jnp.int32, (NV * NV, NV * NV), 0)
        from_row = lax.broadcasted_iota(jnp.int32, (NV * NV, NV * NV), 1)
        v, place = to_row & 15, to_row >> 4
        w = (place & 1) * 8 + ((place >> 1) & 3) * 2 + (place >> 3)
        order = (from_row == v * NV + w).astype(F32).astype(BF16)
        val = dot(order, val_all[q].reshape(NV * NV, 1024)).astype(BF16)
        val_re, val_im = val[:, :512], val[:, 512:]
        scr_re, scr_im = weights[q, :512, :], weights[q, 512:, :]
        real_hi, real_lo = two_terms(dot(val_re, scr_re) - dot(val_im, scr_im))
        imag_hi, imag_lo = two_terms(dot(val_re, scr_im) + dot(val_im, scr_re))
        for ref, real, imag in ((left_hi, real_hi, imag_hi), (left_lo, real_lo, imag_lo)):
            ref[q, 0, :, :512] = real
            ref[q, 0, :, 512:] = -imag
            ref[q, 1, :, :512] = imag
            ref[q, 1, :, 512:] = real

    def core_copy(q, p):
        other = pl.ds(pl.multiple_of((1 - core) * 128, 128), 128)
        return remote(
            direct.at[q, p, other, :], from_core.at[q, p], core_send.at[q, p], core_recv.at[q, p], other_core
        )

    def contract(q):
        con_rest(q)
        for owner in range(16):
            for p in range(2):
                con_rows[owner * 36 : (owner + 1) * 36, p * 512 : (p + 1) * 512] = con_all[
                    owner, q, p * 36 : (p + 1) * 36, :
                ]
        for p in range(2):
            direct[q, p] = dot_rows(left_hi[q, p], con_rows[...]) + dot_rows(left_lo[q, p], con_rows[...])
            start(core_copy(q, p))

    def x_copy(q, p, slot, rows_for, to):
        rows = pl.ds(pl.multiple_of(core * 128 + turn(x, rows_for) * 32, 32), 32)
        return remote(
            direct.at[q, p, rows, :], from_x.at[q, slot, p],
            x_send.at[q, p, slot], x_recv.at[q, p, slot], x_peers[to - 1],
        )

    def to_side(q, p, side):
        return x_copy(q, p, side, 3 if side else 1, 3 if side else 1)

    def by_side(q, p):
        return x_copy(q, p, 2, 2, 3 if p else 1)

    def add_core(q):
        own = pl.ds(pl.multiple_of(core * 128, 128), 128)
        for p in range(2):
            core_copy(q, p).wait_recv()
            direct[q, p, own, :] = direct[q, p, own, :] + from_core[q, p]
            start(by_side(q, p))
        for p in range(2):
            start(to_side(q, p, 1 - p))

    def relay(q):
        for p in range(2):
            by_side(q, p).wait_recv()
            rows = pl.ds(pl.multiple_of(core * 128 + turn(x, 3 if p else 1) * 32, 32), 32)
            direct[q, p, rows, :] = direct[q, p, rows, :] + from_x[q, 2, p]
            start(to_side(q, p, p))

    def row_copy(q, k):
        d, c = row_steps[k]
        rows = pl.ds(pl.multiple_of((turn(x, d) * 2 + lax.rem(core + c, 2)) * 48, 8), 48)
        return remote(
            moved.at[q, rows, :], from_rows.at[q, x * 2 + core], row_send.at[q, k], row_recv.at[q, x * 2 + core],
            row_peers[k],
        )

    def permute_rows(q):
        for p in range(2):
            for copy in [to_side(q, p, k) for k in (0, 1)]:
                copy.wait_recv()
            for half in range(2):
                rows = pl.ds(pl.multiple_of(core * 128 + x * 32 + half * NV, 16), NV)
                block = slice(half * NV, (half + 1) * NV)
                tile = direct[q, p, rows, :] + from_x[q, 0, p, block] + from_x[q, 1, p, block]
                lane = half * 48 + p * NC
                for c in range(NC):
                    parts[c * NV : (c + 1) * NV, lane : lane + NC] = tile[:, c * NC : (c + 1) * NC]
        high, low = two_terms(parts[...])
        moved[q] = exch_moved[q] - dot(rows_sel[...], high) - dot(rows_sel[...], low)
        for k in (1, 0, 2, 5, 4, 6, 3):
            start(row_copy(q, k))
        from_rows[q, x * 2 + core] = moved[q, pl.ds(pl.multiple_of((x * 2 + core) * 48, 8), 48), :]

    def y_copy(q, d):
        rows = pl.ds(pl.multiple_of(turn(y, d) * 96, 32), 96)
        return remote(
            cols.at[q, rows, :], from_y.at[q, d - 1], y_send.at[q, d - 1], y_recv.at[q, d - 1], y_peers[d - 1]
        )

    def permute_cols(q):
        for k, (d, c) in enumerate(row_steps):
            slot = from_rows.at[q, turn(x, d) * 2 + lax.rem(core + c, 2)]
            recv = row_recv.at[q, turn(x, d) * 2 + lax.rem(core + c, 2)]
            remote(slot, slot, row_send.at[q, k], recv, row_peers[k]).wait_recv()
        for slot in range(8):
            for half in range(2):
                tile = from_rows[q, slot, half * NC : (half + 1) * NC, :]
                for zh_ in range(2):
                    w = zh_ * 8 + slot
                    for p in range(2):
                        lane, row = zh_ * 48 + p * NC, half * 48 + p * NC
                        whole[row : row + NC, w * NC : (w + 1) * NC] = tile[:, lane : lane + NC]
        high, low = two_terms(whole[...])
        cols[q] = dot_rows(cols_sel[...], high) + dot_rows(cols_sel[...], low)
        for d in (2, 1, 3):
            start(y_copy(q, d))

    def z_copy(q, d):
        rows = pl.ds(pl.multiple_of(lax.rem(z_to[d - 1], 4) * NC, 8), NC)
        return remote(
            slab.at[q, rows, :], from_z.at[q, d - 1], z_send.at[q, d - 1], z_recv.at[q, d - 1], z_peers[d - 1]
        )

    def add_y(q):
        for d in (1, 2, 3):
            y_copy(q, d).wait_recv()
        own = pl.ds(pl.multiple_of(y * 96, 32), 96)
        slab[q] = cols[q, own, :] + from_y[q, 0] + from_y[q, 1] + from_y[q, 2]
        for d in (4, 3, 5, 2, 6, 1, 7):
            start(z_copy(q, d))

    def add_z(q):
        total = slab[q, pl.ds(pl.multiple_of(zl * NC, 8), NC), :]
        for d in range(1, 8):
            z_copy(q, d).wait_recv()
        for d in range(7):
            total = total + from_z[q, d]
        out_ref[:, q * 48 : (q + 1) * 48] = jnp.where(zh == 0, total[:, :48], total[:, 48:])

    def select():
        places = jnp.transpose(jnp.broadcast_to(places_ref[...].astype(F32)[None, :], (GBLK, NT))).astype(jnp.int32)
        lanes = lax.broadcasted_iota(jnp.int32, (NT, GBLK), 1)

        def block(k):
            return places[k * NC : (k + 1) * NC]

        by_rows = jnp.concatenate([block(zh_ * 8 + s) for s in range(8) for zh_ in range(2)], axis=0)
        by_cols = jnp.concatenate([block(zl_ * 4 + y_) for y_ in range(4) for zl_ in range(4)], axis=0)
        band = jnp.zeros((NT, GBLK), jnp.int32)
        for step in range(1, NV):
            band = band + (by_rows >= step * NC).astype(jnp.int32)
        swapped = (by_rows - band * NC) * NV + band

        def onehot(which):
            parts_ = [(which == lanes + n * GBLK).astype(F32) for n in range(3)]
            return jnp.concatenate(parts_, axis=1).astype(BF16)

        rows_sel[...] = onehot(swapped)
        cols_sel[...] = onehot(by_cols)
        return onehot(by_rows)

    def exchange():
        by_rows = select()
        gather_rest("here")
        for v in range(NV):
            here_rows[v * NC : (v + 1) * NC, :] = here_all[v]
        loads[3].wait()
        highs, lows = [], []
        for q in range(KSEL):
            coul = coul_ref[pl.ds(q, 1), :]
            real_hi, real_lo = two_terms(there_raw[:, q, 0, :].astype(F32) * coul)
            imag_hi, imag_lo = two_terms(there_raw[:, q, 1, :].astype(F32) * coul)
            for out, real, imag in ((highs, real_hi, imag_hi), (lows, real_lo, imag_lo)):
                real, imag = real.astype(F32), imag.astype(F32)
                out.append(jnp.concatenate([real, -imag], axis=1))
                out.append(jnp.concatenate([imag, real], axis=1))
        highs = jnp.concatenate(highs, axis=0).astype(BF16)
        lows = jnp.concatenate(lows, axis=0).astype(BF16)
        high, low = two_terms(dot_rows(here_rows[...], highs) + dot_rows(here_rows[...], lows))
        ordered = 2.0 * (dot(by_rows, high) + dot(by_rows, low))
        for q in range(KSEL):
            tile = ordered[:, q * 48 : (q + 1) * 48]
            exch_moved[q, :, 0:48] = jnp.where(zh == 0, tile, 0.0)
            exch_moved[q, :, 48:96] = jnp.where(zh == 1, tile, 0.0)

    spread_own(0)
    con_line(0)
    con_z(1)
    con_y(0)
    con_y(1)
    con_y(2)
    unshift_weights(0)
    con_from_line(0, 0)
    spread_zh(0)
    con_from_line(0, 1)
    con_z(2)
    spread_own(1)
    spread_x(0, zh)
    con_from_line(0, 2)
    spread_own(2)
    spread_x(0, 1 - zh)
    con_from_z(1, 1)
    spread_own("here")
    gather_rest(0)
    rows_of(0)
    con_from_y(0)
    spread_zh(1)
    con_from_z(1, 2)
    con_from_z(2, 1)
    spread_x(1, zh)
    spread_zh(2)
    spread_x(1, 1 - zh)
    con_from_z(1, 3)
    spread_x(2, zh)
    spread_zh("here")
    contract(0)
    con_from_y(1)
    con_from_z(2, 2)
    add_core(0)
    spread_x(2, 1 - zh)
    spread_x("here", zh)
    con_from_z(2, 3)
    unshift_weights(1)
    unshift_weights(2)
    spread_x("here", 1 - zh)
    gather_rest(1)
    rows_of(1)
    gather_rest(2)
    rows_of(2)
    exchange()
    relay(0)
    con_from_y(2)
    contract(1)
    add_core(1)
    permute_rows(0)
    contract(2)
    relay(1)
    add_core(2)
    permute_cols(0)
    relay(2)
    permute_rows(1)
    permute_rows(2)
    add_y(0)
    permute_cols(1)
    permute_cols(2)
    add_y(1)
    add_z(0)
    add_y(2)
    add_z(1)
    add_z(2)
    for copy, when in maybe:
        pl.when(when)(copy.wait_send)
    for copy in pending:
        copy.wait_send()


def kernel_tiles(con, val, here, there, scr, coul, shift, places):
    any_space = pl.BlockSpec(memory_space=pl.ANY)
    vmem = pl.BlockSpec(memory_space=pltpu.VMEM)
    dma = pltpu.SemaphoreType.DMA
    return pl.pallas_call(
        tiles_kernel,
        name="kernel_tiles",
        out_shape=jax.ShapeDtypeStruct((NC, KSEL * 2 * NC), F32),
        in_specs=[any_space] * 5 + [vmem] * 3,
        out_specs=vmem,
        scratch_shapes=[
            pltpu.VMEM(con.shape, BF16),
            pltpu.VMEM(val.shape, BF16),
            pltpu.VMEM(here.shape, BF16),
            pltpu.VMEM(there.shape, BF16),
            pltpu.VMEM((16, KSEL, 72, 512), BF16),
            pltpu.VMEM((KSEL, 16, NV, 1024), BF16),
            pltpu.VMEM((16, NC, 1024), BF16),
            pltpu.VMEM((NT, 1024), BF16),
            pltpu.VMEM((KSEL, 1024, 512), BF16),
            pltpu.VMEM((NC * NC, 1024), BF16),
            pltpu.VMEM((KSEL, 2, NV * NV, 1024), BF16),
            pltpu.VMEM((KSEL, 2, NV * NV, 1024), BF16),
            pltpu.VMEM((KSEL, 2, NV * NV, NC * NC), F32),
            pltpu.VMEM((KSEL, 2, 128, NC * NC), F32),
            pltpu.VMEM((KSEL, 3, 2, 32, NC * NC), F32),
            pltpu.VMEM((NT, NT), BF16),
            pltpu.VMEM((NT, NT), BF16),
            pltpu.VMEM((KSEL, NT, 96), F32),
            pltpu.VMEM((NT, 96), F32),
            pltpu.VMEM((KSEL, NT, 96), F32),
            pltpu.VMEM((KSEL, 8, 48, 96), F32),
            pltpu.VMEM((96, NT), F32),
            pltpu.VMEM((KSEL, NT, 96), F32),
            pltpu.VMEM((KSEL, 3, 96, 96), F32),
            pltpu.VMEM((KSEL, 96, 96), F32),
            pltpu.VMEM((KSEL, 7, NC, 96), F32),
            dma((72,)), dma((16, KSEL)), dma((KSEL, 16)), dma((KSEL, 16)), dma((16,)), dma((16,)),
            dma((KSEL, 2)), dma((KSEL, 2)), dma((KSEL, 2, 3)), dma((KSEL, 2, 3)), dma((KSEL, 7)), dma((KSEL, 8)),
            dma((KSEL, 3)), dma((KSEL, 3)), dma((KSEL, 7)), dma((KSEL, 7)), dma((7,)),
        ],
        compiler_params=pltpu.CompilerParams(
            collective_id=0, has_side_effects=True, vmem_limit_bytes=60 * 2**20
        ),
    )(con, val, here, there, scr, coul, shift, places)


def on_device(
    val_density, con_density, screened, coulomb, trans_here, trans_there, shift_map, ordering
):
    tiles = kernel_tiles(
        con_density, val_density, trans_here, trans_there, screened.reshape(KSEL, 1024, 512),
        coulomb, shift_map, ordering,
    )
    return jnp.transpose(tiles.reshape(NC, KSEL, 2, NC), (1, 2, 3, 0))


def solution(mesh):
    in_specs = (
        P("pair", None, None, "ga"),
        P("ga", None, None, "pair"),
        P(None, None, "ga", "pair"),
        P(None, "ga"),
        P("pair", None, "ga"),
        P("pair", None, None, "ga"),
        P(None, "pair"),
        P(),
    )
    out_specs = P(None, None, "pair", "ga")
    return jax.shard_map(
        on_device, mesh=mesh, in_specs=in_specs, out_specs=out_specs, check_vma=False
    )
```
